256 devices in a mesh: sub: 128 (over x, y, z), blk: 2 (over core).
Axes of the slice: x: 4, y: 4, z: 8, core: 2. Of those that a mesh axis runs over, the one named last changes fastest.
Arguments:
- basis: bfloat16 [65536, 256], P('sub'), may hold values from -6 to 6
- stiffness: bfloat16 [256, 1024, 1024], P('sub', 'blk')
- mass: bfloat16 [256, 1024, 1024], P('sub', 'blk')
- owner_rows: int32 [128, 128, 16], P('sub'), may hold values from 0 to 511
- counts: int32 [256], P('sub'), may hold values from 256 to 1024, as said below
Outputs:
- rotated: float32 [65536, 256], P(('sub', 'blk'))
- projected: float32 [256, 256], replicated
The draws below stay inside these ranges and needn't reach their ends.
Inputs may be any that keep to these rules, and one draw needn't show every extreme that they name: `counts`: every count lies in 256 to 1024; at least one substructure has all 1024 slots live.
All inputs are finite; a program needn't handle non-finite values.
Results may differ from the reference program's by a relative error of at most 0.002.
Values may be sent and summed in bfloat16 or wider, within the bound.
No kernel may reach another device: no remote copies, remote signals or barrier semaphores. Data moves between devices by JAX's collectives and lax.ppermute only.
A program may use at most 64 MiB of HBM per device.

```python
import math
import jax
import jax.numpy as jnp
from jax import lax

R = 256
NLOC = 1024
SUB_DEV = 2
SUBS = 256
ROWS_DEV = 512
N_IF = 65536
CAP = 16
N_SUB = 128


def block_draw(key, diag_level):
    first, second = jax.random.split(key)
    noise = jax.random.normal(first, (SUBS, NLOC, NLOC), jnp.float32)
    scales = jnp.exp(jax.random.uniform(second, (SUBS, NLOC, 1), jnp.float32, 0.0, 2.302585))
    rise = 1.0 + 2.0 * jnp.arange(SUBS, dtype=jnp.float32) / max(SUBS - 1, 1)
    eye = (jnp.arange(NLOC)[:, None] == jnp.arange(NLOC)[None, :]).astype(jnp.float32)
    return scales * rise[:, None, None] * (diag_level * eye + 0.5 * noise / jnp.sqrt(jnp.float32(NLOC)))


def draw_stiffness(key, part):
    return block_draw(jax.random.fold_in(key, 11), 1.0).astype(jnp.bfloat16)


def draw_mass(key, part):
    return block_draw(jax.random.fold_in(key, 23), 2.0).astype(jnp.bfloat16)


def draw_counts(key, part):
    first, second = jax.random.split(jax.random.fold_in(key, 5))
    values = jax.random.randint(first, (SUBS,), NLOC // 4, NLOC + 1)
    chosen = jax.random.randint(second, (), 0, SUBS)
    return jnp.where(jnp.arange(SUBS) == chosen, NLOC, values).astype(jnp.int32)


def set_ends(array, rng, smallest, top_value):
    spot = [jax.random.randint(jax.random.fold_in(rng, axis), (), 0, length) for axis, length in enumerate(array.shape)]
    longest = array.shape.index(max(array.shape))
    beside = spot[:longest] + [(spot[longest] + 1) % array.shape[longest]] + spot[longest + 1:]
    return array.at[tuple(spot)].set(smallest).at[tuple(beside)].set(top_value)


def levels(stream_key, dims, pieces, least, largest):
    gain, own = 1.0, jax.random.fold_in(stream_key, 6)
    for dim, shards_of in pieces:
        steps = jnp.exp(jax.random.uniform(jax.random.fold_in(own, dim), (shards_of,), jnp.float32, least / len(pieces), largest / len(pieces)))
        gain = gain * jnp.repeat(steps, dims[dim] // shards_of).reshape([-1 if axis == dim else 1 for axis in range(len(dims))])
    return gain


def scatter_about(stream_key, shape, width, reach, cuts=(), kind=jnp.bfloat16):
    entries = width * jax.random.normal(stream_key, shape, jnp.float32)
    if cuts:
        entries = entries * levels(stream_key, shape, cuts, -0.22, 0.18)
    return jnp.clip(entries, -reach, reach).astype(kind)


def setup_inputs(seed: int = 0) -> dict:
    arg_keys = jax.random.split(jax.random.key(seed), 6)
    basis = scatter_about(arg_keys[0], (N_IF, R), 1.0, 6.0, ((0, 128),))
    stiffness = draw_stiffness(jax.random.fold_in(arg_keys[5], 71), 0)
    mass = draw_mass(jax.random.fold_in(arg_keys[5], 71), 0)
    owner_rows = set_ends(jax.random.randint(arg_keys[3], (N_SUB, N_SUB, CAP), 0, ROWS_DEV), jax.random.fold_in(arg_keys[3], 1), 0, ROWS_DEV - 1).astype(jnp.int32)
    counts = draw_counts(jax.random.fold_in(arg_keys[5], 71), 0)
    return dict(basis=basis, stiffness=stiffness, mass=mass, owner_rows=owner_rows, counts=counts)


def slot_rows(t, owner_rows):
    half = NLOC // 2
    cap_half = CAP // 2
    dev = t // SUB_DEV
    local = t % SUB_DEV
    slots = jnp.arange(NLOC, dtype=jnp.int32)
    side = slots // half
    inner = slots % half
    flat = local * half + inner
    owner = (dev + flat) % N_SUB
    place = side * cap_half + flat // N_SUB
    return (owner * ROWS_DEV + owner_rows[owner, dev, place]).astype(jnp.int32)

def reference(basis, stiffness, mass, owner_rows, counts):
    zeros = jnp.zeros((N_IF, R), jnp.float32)

    def step(carry, t):
        image_k, image_m = carry
        index = slot_rows(t, owner_rows)
        live = (jnp.arange(NLOC, dtype=jnp.int32) < counts[t])[:, None]
        local_basis = jnp.where(live, basis[index], jnp.zeros((), jnp.bfloat16))
        stiff_part = jnp.where(live, jnp.dot(stiffness[t].astype(jnp.float32), local_basis.astype(jnp.float32), preferred_element_type=jnp.float32), 0.0).astype(jnp.bfloat16)
        mass_part = jnp.where(live, jnp.dot(mass[t].astype(jnp.float32), local_basis.astype(jnp.float32), preferred_element_type=jnp.float32), 0.0).astype(jnp.bfloat16)
        image_k = image_k.at[index].add(stiff_part.astype(jnp.float32))
        image_m = image_m.at[index].add(mass_part.astype(jnp.float32))
        return ((image_k, image_m), None)
    (image_k, image_m), _ = lax.scan(step, (zeros, zeros), jnp.arange(SUBS, dtype=jnp.int32))
    wide = basis.astype(jnp.float32).T
    gram_k = jnp.dot(wide, image_k, precision=lax.Precision.HIGHEST)
    gram_m = jnp.dot(wide, image_m, precision=lax.Precision.HIGHEST)
    gram_m = 0.5 * (gram_m + gram_m.T)
    lower = jnp.linalg.cholesky(gram_m)
    inverse = lax.linalg.triangular_solve(lower, jnp.eye(R, dtype=lower.dtype), left_side=True, lower=True)
    rotated = math.sqrt(N_IF) * jnp.dot(image_k, inverse.T, precision=lax.Precision.HIGHEST)
    projected = jnp.dot(jnp.dot(inverse, gram_k, precision=lax.Precision.HIGHEST), inverse.T, precision=lax.Precision.HIGHEST)
    return (rotated, projected)
```

```python
import math

import jax
import jax.numpy as jnp
from jax import lax
from jax.sharding import PartitionSpec as P

SWAP = ((0, 1), (1, 0))


def select_rows(index, count):
    places = lax.broadcasted_iota(jnp.int32, (index.shape[0], count), 1)
    return (index[:, None] == places).astype(jnp.bfloat16)


def sum_over_devices(parts, me_blk):
    n, rows, width = parts.shape
    n_sub = lax.axis_size("sub")
    halves = parts.reshape(n, 2, rows // 2, width)
    mine = lax.dynamic_index_in_dim(halves, me_blk, 1, keepdims=False)
    theirs = lax.dynamic_index_in_dim(halves, 1 - me_blk, 1, keepdims=False)
    mine = mine + lax.ppermute(theirs, "blk", SWAP)
    pieces = mine.reshape(n_sub, n * rows // 2 // n_sub, width)
    pieces = lax.all_to_all(pieces, "sub", split_axis=0, concat_axis=0, tiled=True)
    total = jnp.sum(pieces, axis=0)
    spread = jnp.broadcast_to(total[None], pieces.shape)
    mine = lax.all_to_all(spread, "sub", split_axis=0, concat_axis=0, tiled=True)
    mine = mine.reshape(n, rows // 2, width)
    other = lax.ppermute(mine, "blk", SWAP)
    low = jnp.where(me_blk == 0, mine, other)
    high = jnp.where(me_blk == 0, other, mine)
    return jnp.concatenate([low, high], axis=1)


def per_device(basis, stiffness, mass, owner_rows, counts):
    n_sub = lax.axis_size("sub")
    me_sub = lax.axis_index("sub")
    me_blk = lax.axis_index("blk")
    rows_dev, width = basis.shape
    sub_dev, half, order = stiffness.shape
    cap = owner_rows.shape[2]
    cap_half = cap // 2
    table = lax.dynamic_slice_in_dim(owner_rows[0], me_blk * cap_half, cap_half, 1)
    picks = select_rows(table.reshape(-1), rows_dev)

    sent = jnp.dot(picks, basis, preferred_element_type=jnp.float32).astype(jnp.bfloat16)
    received = lax.all_to_all(
        sent.reshape(n_sub, cap_half, width), "sub", split_axis=0, concat_axis=0, tiled=True
    )
    mine = jnp.roll(received, -me_sub, axis=0).transpose(1, 0, 2).reshape(sub_dev, half, width)
    slots = me_blk * half + jnp.arange(half, dtype=jnp.int32)
    my_live = (slots[None, :] < counts[:, None])[:, :, None]
    mine = jnp.where(my_live, mine, jnp.zeros((), jnp.bfloat16))
    other = lax.ppermute(mine, "blk", SWAP)
    low = jnp.where(me_blk == 0, mine, other)
    high = jnp.where(me_blk == 0, other, mine)
    local_basis = jnp.concatenate([low, high], axis=1)

    def product(matrix):
        full = jnp.einsum("sij,sjr->sir", matrix, local_basis, preferred_element_type=jnp.float32)
        return jnp.where(my_live, full, 0.0).astype(jnp.bfloat16)

    stiff_part = product(stiffness)
    mass_part = product(mass)

    def gram(part):
        return jnp.einsum("sir,sic->rc", mine, part, preferred_element_type=jnp.float32)

    grams = sum_over_devices(jnp.stack([gram(stiff_part), gram(mass_part)]), me_blk)
    gram_k, gram_m = grams[0], grams[1]

    outgoing = stiff_part.reshape(cap_half, n_sub, width).transpose(1, 0, 2)
    back = lax.all_to_all(
        jnp.roll(outgoing, me_sub, axis=0), "sub", split_axis=0, concat_axis=0, tiled=True
    )
    image = jnp.einsum(
        "tr,tc->rc", picks, back.reshape(-1, width), preferred_element_type=jnp.float32
    ).reshape(2, rows_dev // 2, width)
    image_k = lax.dynamic_index_in_dim(image, me_blk, 0, keepdims=False) + lax.ppermute(
        lax.dynamic_index_in_dim(image, 1 - me_blk, 0, keepdims=False), "blk", SWAP
    )

    gram_m = 0.5 * (gram_m + gram_m.T)
    lower = jnp.linalg.cholesky(gram_m)
    inverse = lax.linalg.triangular_solve(
        lower, jnp.eye(width, dtype=lower.dtype), left_side=True, lower=True
    )
    scale_rows = math.sqrt(rows_dev * n_sub)
    rotated = scale_rows * jnp.dot(image_k, inverse.T, precision=lax.Precision.HIGH)
    projected = jnp.dot(
        jnp.dot(inverse, gram_k, precision=lax.Precision.HIGHEST),
        inverse.T,
        precision=lax.Precision.HIGHEST,
    )
    return (rotated, projected)


def solution(mesh):
    return jax.shard_map(
        per_device,
        mesh=mesh,
        in_specs=(
            P("sub", None),
            P("sub", "blk", None),
            P("sub", "blk", None),
            P("sub", None, None),
            P("sub"),
        ),
        out_specs=(P(("sub", "blk"), None), P()),
        check_vma=False,
    )
```

```python
import math

import jax
import jax.numpy as jnp
from jax import lax
from jax.experimental import pallas as pl
from jax.experimental.pallas import tpu as pltpu
from jax.sharding import PartitionSpec as P

SWAP = ((0, 1), (1, 0))
MAX_STEPS = 7
RESIDUAL = 2.5e-7
HIGHEST = lax.Precision.HIGHEST


def select_rows(index, count):
    places = lax.broadcasted_iota(jnp.int32, (index.shape[0], count), 1)
    return (index[:, None] == places).astype(jnp.bfloat16)


def two_terms(value):
    upper = lax.reduce_precision(value, exponent_bits=8, mantissa_bits=7)
    return upper.astype(jnp.bfloat16), (value - upper).astype(jnp.bfloat16)


def mat(left, right):
    return lax.dot_general(
        left, right, (((1,), (0,)), ((), ())), precision=HIGHEST, preferred_element_type=jnp.float32
    )


def mat_t(left, right):
    return lax.dot_general(
        left, right, (((1,), (1,)), ((), ())), precision=HIGHEST, preferred_element_type=jnp.float32
    )


def ritz_kernel(gram_m_ref, gram_k_ref, inverse_ref, projected_ref, good_ref, sym_ref):
    n = gram_m_ref.shape[0]
    row = lax.broadcasted_iota(jnp.int32, (n, n), 0)
    col = lax.broadcasted_iota(jnp.int32, (n, n), 1)
    weight = jnp.where(row > col, 1.0, jnp.where(row == col, 0.5, 0.0))
    gram = gram_m_ref[...]
    gram = 0.5 * (gram + gram.T)
    sym_ref[...] = gram
    on_diag = jnp.where(row == col, gram, 0.0)
    down = lax.rsqrt(jnp.sum(on_diag, axis=1, keepdims=True))
    across = lax.rsqrt(jnp.sum(on_diag, axis=0, keepdims=True))
    error = gram * down * across - jnp.where(row == col, 1.0, 0.0)
    inverse_ref[...] = (jnp.where(row == col, 1.0, 0.0) - weight * error) * across

    def going(state):
        step, size = state
        return jnp.logical_and(step < MAX_STEPS, jnp.logical_not(size < RESIDUAL))

    def correct(state):
        step, _ = state
        inverse = inverse_ref[...]
        error = mat_t(mat(inverse, sym_ref[...]), inverse) - jnp.where(row == col, 1.0, 0.0)
        inverse_ref[...] = inverse - mat(weight * error, inverse)
        return step + 1, jnp.sum(error * error)

    _, size = lax.while_loop(going, correct, (jnp.int32(0), jnp.float32(1.0)))
    good_ref[0, 0] = jnp.where(size < RESIDUAL, 1, 0).astype(jnp.int32)
    inverse = inverse_ref[...]
    projected_ref[...] = mat_t(mat(inverse, gram_k_ref[...]), inverse)


def ritz(gram_m, gram_k):
    n = gram_m.shape[0]
    vmem = pl.BlockSpec(memory_space=pltpu.VMEM)
    inverse, projected, good = pl.pallas_call(
        ritz_kernel,
        out_shape=(
            jax.ShapeDtypeStruct((n, n), jnp.float32),
            jax.ShapeDtypeStruct((n, n), jnp.float32),
            jax.ShapeDtypeStruct((1, 1), jnp.int32),
        ),
        in_specs=[vmem, vmem],
        out_specs=(vmem, vmem, pl.BlockSpec(memory_space=pltpu.SMEM)),
        scratch_shapes=[pltpu.VMEM((n, n), jnp.float32)],
        name="ritz",
    )(gram_m, gram_k)

    def direct():
        lower = jnp.linalg.cholesky(0.5 * (gram_m + gram_m.T))
        solved = lax.linalg.triangular_solve(
            lower, jnp.eye(n, dtype=lower.dtype), left_side=True, lower=True
        )
        middle = jnp.dot(solved, gram_k, precision=HIGHEST)
        return solved, jnp.dot(middle, solved.T, precision=HIGHEST)

    return lax.cond(good[0, 0] > 0, lambda: (inverse, projected), direct)


def to_pieces(plane):
    rows, wide = plane.shape
    return plane.reshape(rows // 2, 2, 2, wide // 2).transpose(2, 0, 1, 3).reshape(rows, 2, wide // 2)


def from_pieces(pieces):
    rows, _, lanes = pieces.shape
    return pieces.reshape(2, rows // 2, 2, lanes).transpose(1, 2, 0, 3).reshape(rows, 2 * lanes)


def per_device(basis, stiffness, mass, owner_rows, counts):
    n_sub = lax.axis_size("sub")
    me_sub = lax.axis_index("sub")
    me_blk = lax.axis_index("blk")
    rows_dev, width = basis.shape
    sub_dev, half, order = stiffness.shape
    cap = owner_rows.shape[2]
    cap_half = cap // 2
    lanes = width // 2
    table = lax.dynamic_slice_in_dim(owner_rows[0], me_blk * cap_half, cap_half, 1)
    picks = select_rows(table.reshape(-1), rows_dev)

    sent = jnp.dot(picks, basis, preferred_element_type=jnp.float32).astype(jnp.bfloat16)
    received = lax.all_to_all(
        sent.reshape(n_sub, cap_half, width), "sub", split_axis=0, concat_axis=0, tiled=True
    )
    mine = jnp.roll(received, -me_sub, axis=0).transpose(1, 0, 2).reshape(sub_dev, half, width)
    slots = me_blk * half + jnp.arange(half, dtype=jnp.int32)
    my_live = (slots[None, :] < counts[:, None])[:, :, None]
    mine = jnp.where(my_live, mine, jnp.zeros((), jnp.bfloat16))
    other = lax.ppermute(mine, "blk", SWAP)
    low = jnp.where(me_blk == 0, mine, other)
    high = jnp.where(me_blk == 0, other, mine)
    local_basis = jnp.concatenate([low, high], axis=1)

    def product(matrix):
        full = jnp.einsum("sij,sjr->sir", matrix, local_basis, preferred_element_type=jnp.float32)
        return jnp.where(my_live, full, 0.0).astype(jnp.bfloat16)

    stiff_part = product(stiffness)
    mass_part = product(mass)

    def gram(part):
        return jnp.einsum("sir,sic->rc", mine, part, preferred_element_type=jnp.float32)

    grams = jnp.stack([gram(mass_part), gram(stiff_part)]).reshape(2, 2, width // 2, width)
    grams = lax.dynamic_index_in_dim(grams, me_blk, 1, keepdims=False) + lax.ppermute(
        lax.dynamic_index_in_dim(grams, 1 - me_blk, 1, keepdims=False), "blk", SWAP
    )
    terms = [to_pieces(term) for plane in (grams[0], grams[1]) for term in two_terms(plane)]
    outgoing = stiff_part.reshape(cap_half, n_sub, width).transpose(1, 0, 2)
    outgoing = jnp.roll(outgoing, me_sub, axis=0)
    back = lax.all_to_all(
        jnp.concatenate([outgoing, jnp.concatenate(terms, axis=1)], axis=2),
        "sub",
        split_axis=0,
        concat_axis=0,
        tiled=True,
    )
    total = jnp.sum(back[:, :, width:].astype(jnp.float32), axis=0).reshape(2, 2, 2, lanes)
    total = jnp.sum(total, axis=1).reshape(4, lanes)
    spread = lax.all_to_all(
        jnp.broadcast_to(total[None], (n_sub, 4, lanes)),
        "sub",
        split_axis=0,
        concat_axis=0,
        tiled=True,
    )
    mine_grams = jnp.stack([from_pieces(spread[:, :2]), from_pieces(spread[:, 2:])])
    other_grams = lax.ppermute(mine_grams, "blk", SWAP)
    grams = jnp.concatenate(
        [
            jnp.where(me_blk == 0, mine_grams, other_grams),
            jnp.where(me_blk == 0, other_grams, mine_grams),
        ],
        axis=1,
    )

    image = jnp.einsum(
        "tr,tc->rc",
        picks,
        back[:, :, :width].reshape(-1, width),
        preferred_element_type=jnp.float32,
    ).reshape(2, rows_dev // 2, width)
    image_k = lax.dynamic_index_in_dim(image, me_blk, 0, keepdims=False) + lax.ppermute(
        lax.dynamic_index_in_dim(image, 1 - me_blk, 0, keepdims=False), "blk", SWAP
    )

    inverse, projected = ritz(grams[0], grams[1])
    scale_rows = math.sqrt(rows_dev * n_sub)
    rotated = scale_rows * jnp.dot(image_k, inverse.T, precision=lax.Precision.HIGH)
    return (rotated, projected)


def solution(mesh):
    return jax.shard_map(
        per_device,
        mesh=mesh,
        in_specs=(
            P("sub", None),
            P("sub", "blk", None),
            P("sub", "blk", None),
            P("sub", None, None),
            P("sub"),
        ),
        out_specs=(P(("sub", "blk"), None), P()),
        check_vma=False,
    )
```

```python
import functools
import math

import jax
import jax.numpy as jnp
from jax import lax
from jax.experimental import pallas as pl
from jax.experimental.pallas import tpu as pltpu
from jax.sharding import PartitionSpec as P

SWAP = ((0, 1), (1, 0))
MAX_STEPS = 7
RESIDUAL = 1e-6
HIGHEST = lax.Precision.HIGHEST


def select_rows(index, count):
    places = lax.broadcasted_iota(jnp.int32, (index.shape[0], count), 1)
    return (index[:, None] == places).astype(jnp.bfloat16)


def two_terms(value):
    upper = lax.reduce_precision(value, exponent_bits=8, mantissa_bits=7)
    return upper.astype(jnp.bfloat16), (value - upper).astype(jnp.bfloat16)


def mat(left, right):
    return lax.dot_general(
        left, right, (((1,), (0,)), ((), ())), precision=HIGHEST, preferred_element_type=jnp.float32
    )


def mat_t(left, right):
    return lax.dot_general(
        left, right, (((1,), (1,)), ((), ())), precision=HIGHEST, preferred_element_type=jnp.float32
    )


def short(left, right, side):
    return lax.dot_general(
        left.astype(jnp.bfloat16),
        right.astype(jnp.bfloat16),
        (((1,), (side,)), ((), ())),
        preferred_element_type=jnp.float32,
    )


def product_kernel(counts_ref, mine_ref, other_ref, stiff_ref, mass_ref, part_ref, keep_ref, send_ref):
    sub_dev, half, width = mine_ref.shape
    me_blk = lax.axis_index("blk")
    first = me_blk == 0
    own = pl.ds(pl.multiple_of(me_blk * half, half), half)
    far = pl.ds(pl.multiple_of((1 - me_blk) * half, half), half)
    slot = me_blk * half + lax.broadcasted_iota(jnp.int32, (half, width), 0)
    for place, matrix_ref in enumerate((mass_ref, stiff_ref)):
        gram = None
        for s in range(sub_dev):
            mine = mine_ref[s]
            part = jnp.dot(matrix_ref[s, :, own], mine, preferred_element_type=jnp.float32)
            part += jnp.dot(matrix_ref[s, :, far], other_ref[s], preferred_element_type=jnp.float32)
            part = jnp.where(slot < counts_ref[s], part, 0.0).astype(jnp.bfloat16)
            if place == 1:
                part_ref[s] = part
            term = lax.dot_general(
                mine, part, (((0,), (0,)), ((), ())), preferred_element_type=jnp.float32
            )
            gram = term if gram is None else gram + term
        low, high = gram[: width // 2], gram[width // 2 :]
        keep_ref[place] = jnp.where(first, low, high)
        send_ref[place] = jnp.where(first, high, low)


def products(counts, mine, other, stiffness, mass):
    sub_dev, half, width = mine.shape
    vmem = pl.BlockSpec(memory_space=pltpu.VMEM)
    gram = jax.ShapeDtypeStruct((2, width // 2, width), jnp.float32)
    return pl.pallas_call(
        product_kernel,
        out_shape=(jax.ShapeDtypeStruct(mine.shape, jnp.bfloat16), gram, gram),
        in_specs=[pl.BlockSpec(memory_space=pltpu.SMEM)] + [vmem] * 4,
        out_specs=(vmem, vmem, vmem),
        compiler_params=pltpu.CompilerParams(vmem_limit_bytes=24 << 20),
        cost_estimate=pl.CostEstimate(
            flops=1400000000, bytes_accessed=6 << 20, transcendentals=0
        ),
        name="products",
    )(counts, mine, other, stiffness, mass)


def ritz_kernel(
    scale, mine_ref, other_ref, image_ref, extra_ref, rotated_ref, projected_ref, good_ref, gram_ref, inverse_ref
):
    rows, n = mine_ref.shape[1:]
    me_blk = lax.axis_index("blk")
    gram_ref[0, pl.ds(pl.multiple_of(me_blk * rows, rows), rows), :] = mine_ref[0]
    gram_ref[0, pl.ds(pl.multiple_of((1 - me_blk) * rows, rows), rows), :] = other_ref[0]
    gram_ref[1, pl.ds(pl.multiple_of(me_blk * rows, rows), rows), :] = mine_ref[1]
    gram_ref[1, pl.ds(pl.multiple_of((1 - me_blk) * rows, rows), rows), :] = other_ref[1]
    row = lax.broadcasted_iota(jnp.int32, (n, n), 0)
    col = lax.broadcasted_iota(jnp.int32, (n, n), 1)
    eye = jnp.where(row == col, 1.0, 0.0)
    weight = jnp.where(row > col, 1.0, 0.5 * eye)
    gram = gram_ref[0]
    gram = 0.5 * (gram + gram.T)
    on_diag = eye * gram
    down = lax.rsqrt(jnp.sum(on_diag, axis=1, keepdims=True))
    across = lax.rsqrt(jnp.sum(on_diag, axis=0, keepdims=True))
    scaled = gram * down * across
    gram_ref[0] = scaled
    rest = scaled - eye
    off = -weight * rest
    for _ in range(2):
        left = rest + off + short(off, rest, 0)
        step = weight * (left + off.T + short(left, off, 1))
        off = off - step - short(step, off, 0)
    inverse_ref[...] = eye + off

    def going(state):
        step, size = state
        return jnp.logical_and(step < MAX_STEPS, jnp.logical_not(size < RESIDUAL))

    def correct(state):
        step, _ = state
        inverse = inverse_ref[...]
        error = mat_t(mat(inverse, gram_ref[0]), inverse) - eye
        inverse_ref[...] = inverse - mat(weight * error, inverse)
        return step + 1, jnp.sum(error * error)

    _, size = lax.while_loop(going, correct, (jnp.int32(0), jnp.float32(1.0)))
    good_ref[0, 0] = jnp.where(size < RESIDUAL, 1, 0).astype(jnp.int32)
    inverse = inverse_ref[...] * across
    rotated_ref[...] = scale * mat_t(image_ref[...] + extra_ref[...], inverse)
    projected_ref[...] = mat_t(mat(inverse, gram_ref[1]), inverse)


def ritz(mine, other, image, extra, scale, me_blk):
    rows, n = mine.shape[1:]
    vmem = pl.BlockSpec(memory_space=pltpu.VMEM)
    square = jax.ShapeDtypeStruct((n, n), jnp.float32)
    rotated, projected, good = pl.pallas_call(
        functools.partial(ritz_kernel, scale),
        out_shape=(square, square, jax.ShapeDtypeStruct((1, 1), jnp.int32)),
        in_specs=[vmem] * 4,
        out_specs=(vmem, vmem, pl.BlockSpec(memory_space=pltpu.SMEM)),
        scratch_shapes=[pltpu.VMEM((2, n, n), jnp.float32), pltpu.VMEM((n, n), jnp.float32)],
        name="ritz",
    )(mine, other, image, extra)

    def direct():
        low = jnp.where(me_blk == 0, mine, other)
        high = jnp.where(me_blk == 0, other, mine)
        gram_m, gram_k = jnp.concatenate([low, high], axis=1)
        lower = jnp.linalg.cholesky(0.5 * (gram_m + gram_m.T))
        solved = lax.linalg.triangular_solve(
            lower, jnp.eye(n, dtype=lower.dtype), left_side=True, lower=True
        )
        middle = jnp.dot(solved, gram_k, precision=HIGHEST)
        return (
            scale * jnp.dot(image + extra, solved.T, precision=HIGHEST),
            jnp.dot(middle, solved.T, precision=HIGHEST),
        )

    return lax.cond(good[0, 0] > 0, lambda: (rotated, projected), direct)


def to_pieces(plane):
    rows, wide = plane.shape
    return plane.reshape(rows // 2, 2, 2, wide // 2).transpose(2, 0, 1, 3).reshape(rows, 2, wide // 2)


def from_pieces(pieces):
    rows, _, lanes = pieces.shape
    return pieces.reshape(2, rows // 2, 2, lanes).transpose(1, 2, 0, 3).reshape(rows, 2 * lanes)


def per_device(basis, stiffness, mass, owner_rows, counts):
    n_sub = lax.axis_size("sub")
    me_sub = lax.axis_index("sub")
    me_blk = lax.axis_index("blk")
    rows_dev, width = basis.shape
    sub_dev, half, order = stiffness.shape
    cap = owner_rows.shape[2]
    cap_half = cap // 2
    lanes = width // 2
    table = lax.dynamic_slice_in_dim(owner_rows[0], me_blk * cap_half, cap_half, 1)
    picks = select_rows(table.reshape(-1), rows_dev)

    sent = jnp.dot(picks, basis, preferred_element_type=jnp.float32).astype(jnp.bfloat16)
    received = lax.all_to_all(
        sent.reshape(n_sub, cap_half, width), "sub", split_axis=0, concat_axis=0, tiled=True
    )
    mine = jnp.roll(received, -me_sub, axis=0).transpose(1, 0, 2).reshape(sub_dev, half, width)
    slots = me_blk * half + jnp.arange(half, dtype=jnp.int32)
    my_live = (slots[None, :] < counts[:, None])[:, :, None]
    mine = jnp.where(my_live, mine, jnp.zeros((), jnp.bfloat16))
    other = lax.ppermute(mine, "blk", SWAP)
    stiff_part, keep, send = products(counts, mine, other, stiffness, mass)
    grams = keep + lax.ppermute(send, "blk", SWAP)
    terms = [to_pieces(term) for plane in (grams[0], grams[1]) for term in two_terms(plane)]
    outgoing = stiff_part.reshape(cap_half, n_sub, width).transpose(1, 0, 2)
    outgoing = jnp.roll(outgoing, me_sub, axis=0)
    back = lax.all_to_all(
        jnp.concatenate([outgoing, jnp.concatenate(terms, axis=1)], axis=2),
        "sub",
        split_axis=0,
        concat_axis=0,
        tiled=True,
    )
    total = jnp.sum(back[:, :, width:].astype(jnp.float32), axis=0).reshape(2, 2, 2, lanes)
    total = jnp.sum(total, axis=1).reshape(4, lanes)
    spread = lax.all_to_all(
        jnp.broadcast_to(total[None], (n_sub, 4, lanes)),
        "sub",
        split_axis=0,
        concat_axis=0,
        tiled=True,
    )
    mine_grams = jnp.stack([from_pieces(spread[:, :2]), from_pieces(spread[:, 2:])])
    other_grams = lax.ppermute(mine_grams, "blk", SWAP)
    image = jnp.einsum(
        "tr,tc->rc",
        picks,
        back[:, :, :width].reshape(-1, width),
        preferred_element_type=jnp.float32,
    ).reshape(2, rows_dev // 2, width)
    image_k = lax.dynamic_index_in_dim(image, me_blk, 0, keepdims=False)
    extra_k = lax.ppermute(
        lax.dynamic_index_in_dim(image, 1 - me_blk, 0, keepdims=False), "blk", SWAP
    )
    return ritz(
        mine_grams, other_grams, image_k, extra_k, math.sqrt(rows_dev * n_sub), me_blk
    )


def solution(mesh):
    return jax.shard_map(
        per_device,
        mesh=mesh,
        in_specs=(
            P("sub", None),
            P("sub", "blk", None),
            P("sub", "blk", None),
            P("sub", None, None),
            P("sub"),
        ),
        out_specs=(P(("sub", "blk"), None), P()),
        check_vma=False,
    )
```

```python
import functools
import math

import jax
import jax.numpy as jnp
from jax import lax
from jax.experimental import pallas as pl
from jax.experimental.pallas import tpu as pltpu
from jax.sharding import PartitionSpec as P

SWAP = ((0, 1), (1, 0))
MAX_STEPS = 7
RESIDUAL = 1e-6
HIGHEST = lax.Precision.HIGHEST


def select_rows(index, count):
    places = lax.broadcasted_iota(jnp.int32, (index.shape[0], count), 1)
    return (index[:, None] == places).astype(jnp.bfloat16)


def two_terms(value):
    upper = lax.reduce_precision(value, exponent_bits=8, mantissa_bits=7)
    return upper.astype(jnp.bfloat16), (value - upper).astype(jnp.bfloat16)


def mat(left, right):
    return lax.dot_general(
        left, right, (((1,), (0,)), ((), ())), precision=HIGHEST, preferred_element_type=jnp.float32
    )


def mat_t(left, right):
    return lax.dot_general(
        left, right, (((1,), (1,)), ((), ())), precision=HIGHEST, preferred_element_type=jnp.float32
    )


def short(left, right, side):
    return lax.dot_general(
        left.astype(jnp.bfloat16),
        right.astype(jnp.bfloat16),
        (((1,), (side,)), ((), ())),
        preferred_element_type=jnp.float32,
    )


def product_kernel(counts_ref, mine_ref, other_ref, stiff_ref, mass_ref, part_ref, keep_ref, send_ref):
    sub_dev, half, width = mine_ref.shape
    me_blk = lax.axis_index("blk")
    first = me_blk == 0
    own = pl.ds(pl.multiple_of(me_blk * half, half), half)
    far = pl.ds(pl.multiple_of((1 - me_blk) * half, half), half)
    slot = me_blk * half + lax.broadcasted_iota(jnp.int32, (half, width), 0)
    for place, matrix_ref in enumerate((mass_ref, stiff_ref)):
        gram = None
        for s in range(sub_dev):
            mine = mine_ref[s]
            part = jnp.dot(matrix_ref[s, :, own], mine, preferred_element_type=jnp.float32)
            part += jnp.dot(matrix_ref[s, :, far], other_ref[s], preferred_element_type=jnp.float32)
            part = jnp.where(slot < counts_ref[s], part, 0.0).astype(jnp.bfloat16)
            if place == 1:
                part_ref[s] = part
            term = lax.dot_general(
                mine, part, (((0,), (0,)), ((), ())), preferred_element_type=jnp.float32
            )
            gram = term if gram is None else gram + term
        low, high = gram[: width // 2], gram[width // 2 :]
        keep_ref[place] = jnp.where(first, low, high)
        send_ref[place] = jnp.where(first, high, low)


def products(counts, mine, other, stiffness, mass):
    sub_dev, half, width = mine.shape
    vmem = pl.BlockSpec(memory_space=pltpu.VMEM)
    gram = jax.ShapeDtypeStruct((2, width // 2, width), jnp.float32)
    return pl.pallas_call(
        product_kernel,
        out_shape=(jax.ShapeDtypeStruct(mine.shape, jnp.bfloat16), gram, gram),
        in_specs=[pl.BlockSpec(memory_space=pltpu.SMEM)] + [vmem] * 4,
        out_specs=(vmem, vmem, vmem),
        compiler_params=pltpu.CompilerParams(vmem_limit_bytes=24 << 20),
        cost_estimate=pl.CostEstimate(
            flops=1400000000, bytes_accessed=6 << 20, transcendentals=0
        ),
        name="products",
    )(counts, mine, other, stiffness, mass)


def eliminate(work_ref, inverse_ref):
    n = work_ref.shape[0]
    row = lax.broadcasted_iota(jnp.int32, (n, n), 0)
    col = lax.broadcasted_iota(jnp.int32, (n, n), 1)
    lane = lax.broadcasted_iota(jnp.int32, (1, n), 1)
    inverse_ref[...] = jnp.where(row == col, 1.0, 0.0)

    def column(k, _):
        pivot_row = work_ref[pl.ds(k, 1), :]
        pivot = jnp.sum(jnp.where(lane == k, pivot_row, 0.0), axis=1, keepdims=True)
        work = work_ref[...]
        inverse = inverse_ref[...]
        below = jnp.sum(jnp.where(col == k, work, 0.0), axis=1, keepdims=True) / pivot
        below = jnp.where(row[:, :1] > k, below, 0.0)
        inverse_row = inverse_ref[pl.ds(k, 1), :]
        work_ref[...] = work - below * pivot_row
        inverse = inverse - below * inverse_row
        inverse_ref[...] = jnp.where(row == k, inverse * lax.rsqrt(pivot), inverse)
        return 0

    lax.fori_loop(0, n, column, 0)


def ritz_kernel(
    scale,
    mine_ref,
    other_ref,
    image_ref,
    extra_ref,
    rotated_hbm,
    projected_hbm,
    gram_ref,
    inverse_ref,
    rotated_ref,
    projected_ref,
    sems,
):
    rows, n = mine_ref.shape[1:]
    me_blk = lax.axis_index("blk")
    own = pl.ds(pl.multiple_of(me_blk * rows, rows), rows)
    far = pl.ds(pl.multiple_of((1 - me_blk) * rows, rows), rows)
    for plane in range(2):
        gram_ref[plane, own, :] = mine_ref[plane]
        gram_ref[plane, far, :] = other_ref[plane]
    row = lax.broadcasted_iota(jnp.int32, (n, n), 0)
    col = lax.broadcasted_iota(jnp.int32, (n, n), 1)
    eye = jnp.where(row == col, 1.0, 0.0)
    weight = jnp.where(row > col, 1.0, 0.5 * eye)
    gram = gram_ref[0]
    gram = 0.5 * (gram + gram.T)
    projected_ref[...] = gram
    on_diag = jnp.where(row == col, gram, 0.0)
    down = lax.rsqrt(jnp.sum(on_diag, axis=1, keepdims=True))
    across = lax.rsqrt(jnp.sum(on_diag, axis=0, keepdims=True))
    scaled = gram * down * across
    gram_ref[0] = scaled
    rest = scaled - eye
    off = -weight * rest
    for _ in range(2):
        left = rest + off + short(off, rest, 0)
        step = weight * (left + off.T + short(left, off, 1))
        off = off - step - short(step, off, 0)
    inverse_ref[...] = eye + off

    def going(state):
        step, size = state
        return jnp.logical_and(step < MAX_STEPS, jnp.logical_not(size < RESIDUAL))

    def correct(state):
        step, _ = state
        inverse = inverse_ref[...]
        error = mat_t(mat(inverse, gram_ref[0]), inverse) - eye
        inverse_ref[...] = inverse - mat(weight * error, inverse)
        return step + 1, jnp.sum(error * error)

    _, size = lax.while_loop(going, correct, (jnp.int32(0), jnp.float32(1.0)))

    inverse_ref[...] = inverse_ref[...] * across

    @pl.when(jnp.logical_not(size < RESIDUAL))
    def _():
        eliminate(projected_ref, inverse_ref)

    inverse = inverse_ref[...]
    rotated_ref[...] = scale * mat_t(image_ref[...] + extra_ref[...], inverse)
    first = pltpu.make_async_copy(rotated_ref, rotated_hbm, sems.at[0])
    first.start()
    projected_ref[...] = mat_t(mat(inverse, gram_ref[1]), inverse)
    second = pltpu.make_async_copy(projected_ref, projected_hbm, sems.at[1])
    second.start()
    first.wait()
    second.wait()


def ritz(mine, other, image, extra, scale):
    n = mine.shape[2]
    vmem = pl.BlockSpec(memory_space=pltpu.VMEM)
    hbm = pl.BlockSpec(memory_space=pltpu.HBM)
    square = jax.ShapeDtypeStruct((n, n), jnp.float32)
    return pl.pallas_call(
        functools.partial(ritz_kernel, scale),
        out_shape=(square, square),
        in_specs=[vmem] * 4,
        out_specs=(hbm, hbm),
        scratch_shapes=[
            pltpu.VMEM((2, n, n), jnp.float32),
            pltpu.VMEM((n, n), jnp.float32),
            pltpu.VMEM((n, n), jnp.float32),
            pltpu.VMEM((n, n), jnp.float32),
            pltpu.SemaphoreType.DMA((2,)),
        ],
        name="ritz",
    )(mine, other, image, extra)


def to_pieces(plane):
    rows, wide = plane.shape
    return plane.reshape(rows // 2, 2, 2, wide // 2).transpose(2, 0, 1, 3).reshape(rows, 2, wide // 2)


def from_pieces(pieces):
    rows, _, lanes = pieces.shape
    return pieces.reshape(2, rows // 2, 2, lanes).transpose(1, 2, 0, 3).reshape(rows, 2 * lanes)


def per_device(basis, stiffness, mass, owner_rows, counts):
    n_sub = lax.axis_size("sub")
    me_sub = lax.axis_index("sub")
    me_blk = lax.axis_index("blk")
    rows_dev, width = basis.shape
    sub_dev, half, order = stiffness.shape
    cap = owner_rows.shape[2]
    cap_half = cap // 2
    lanes = width // 2
    table = lax.dynamic_slice_in_dim(owner_rows[0], me_blk * cap_half, cap_half, 1)
    picks = select_rows(table.reshape(-1), rows_dev)

    sent = jnp.dot(picks, basis, preferred_element_type=jnp.float32).astype(jnp.bfloat16)
    received = lax.all_to_all(
        sent.reshape(n_sub, cap_half, width), "sub", split_axis=0, concat_axis=0, tiled=True
    )
    mine = jnp.roll(received, -me_sub, axis=0).transpose(1, 0, 2).reshape(sub_dev, half, width)
    slots = me_blk * half + jnp.arange(half, dtype=jnp.int32)
    my_live = (slots[None, :] < counts[:, None])[:, :, None]
    mine = jnp.where(my_live, mine, jnp.zeros((), jnp.bfloat16))
    other = lax.ppermute(mine, "blk", SWAP)
    stiff_part, keep, send = products(counts, mine, other, stiffness, mass)
    grams = keep + lax.ppermute(send, "blk", SWAP)
    terms = [to_pieces(term) for plane in (grams[0], grams[1]) for term in two_terms(plane)]
    outgoing = stiff_part.reshape(cap_half, n_sub, width).transpose(1, 0, 2)
    outgoing = jnp.roll(outgoing, me_sub, axis=0)
    back = lax.all_to_all(
        jnp.concatenate([outgoing, jnp.concatenate(terms, axis=1)], axis=2),
        "sub",
        split_axis=0,
        concat_axis=0,
        tiled=True,
    )
    total = jnp.sum(back[:, :, width:].astype(jnp.float32), axis=0).reshape(2, 2, 2, lanes)
    total = jnp.sum(total, axis=1).reshape(4, lanes)
    spread = lax.all_to_all(
        jnp.broadcast_to(total[None], (n_sub, 4, lanes)),
        "sub",
        split_axis=0,
        concat_axis=0,
        tiled=True,
    )
    mine_grams = jnp.stack([from_pieces(spread[:, :2]), from_pieces(spread[:, 2:])])
    other_grams = lax.ppermute(mine_grams, "blk", SWAP)
    image = jnp.einsum(
        "tr,tc->rc",
        picks,
        back[:, :, :width].reshape(-1, width),
        preferred_element_type=jnp.float32,
    ).reshape(2, rows_dev // 2, width)
    image_k = lax.dynamic_index_in_dim(image, me_blk, 0, keepdims=False)
    extra_k = lax.ppermute(
        lax.dynamic_index_in_dim(image, 1 - me_blk, 0, keepdims=False), "blk", SWAP
    )
    return ritz(mine_grams, other_grams, image_k, extra_k, math.sqrt(rows_dev * n_sub))


def solution(mesh):
    return jax.shard_map(
        per_device,
        mesh=mesh,
        in_specs=(
            P("sub", None),
            P("sub", "blk", None),
            P("sub", "blk", None),
            P("sub", None, None),
            P("sub"),
        ),
        out_specs=(P(("sub", "blk"), None), P()),
        check_vma=False,
    )
```

```python
import functools
import math

import jax
import jax.numpy as jnp
from jax import lax
from jax.experimental import pallas as pl
from jax.experimental.pallas import tpu as pltpu
from jax.sharding import PartitionSpec as P

SWAP = ((0, 1), (1, 0))
MAX_STEPS = 7
RESIDUAL = 1e-6


def select_rows(index, count):
    places = lax.broadcasted_iota(jnp.int32, (index.shape[0], count), 1)
    return (index[:, None] == places).astype(jnp.bfloat16)


def two_terms(value):
    upper = lax.reduce_precision(value, exponent_bits=8, mantissa_bits=7)
    return upper.astype(jnp.bfloat16), (value - upper).astype(jnp.bfloat16)


def short(left, right, side):
    return lax.dot_general(
        left.astype(jnp.bfloat16),
        right.astype(jnp.bfloat16),
        (((1,), (side,)), ((), ())),
        preferred_element_type=jnp.float32,
    )


def long(left, right, side):
    left_top = left.astype(jnp.bfloat16)
    left_rest = left - left_top.astype(jnp.float32)
    right_top = right.astype(jnp.bfloat16)
    right_rest = right - right_top.astype(jnp.float32)
    small = short(left_top, right_rest, side) + short(left_rest, right_top, side)
    return small + short(left_top, right_top, side)


def halves(half):
    me_blk = lax.axis_index("blk")
    own = pl.ds(pl.multiple_of(me_blk * half, half), half)
    far = pl.ds(pl.multiple_of((1 - me_blk) * half, half), half)
    return me_blk, own, far


def own_kernel(mine_ref, stiff_ref, mass_ref, partial_ref):
    sub_dev, half, _ = mine_ref.shape
    _, own, _ = halves(half)
    for place, matrix_ref in enumerate((mass_ref, stiff_ref)):
        for s in range(sub_dev):
            partial_ref[place, s] = jnp.dot(
                matrix_ref[s, :, own], mine_ref[s], preferred_element_type=jnp.float32
            )


def far_kernel(
    counts_ref, partial_ref, mine_ref, other_ref, stiff_ref, mass_ref, part_ref, keep_ref, send_ref
):
    sub_dev, half, width = mine_ref.shape
    me_blk, _, far = halves(half)
    first = me_blk == 0
    slot = me_blk * half + lax.broadcasted_iota(jnp.int32, (half, width), 0)
    for place, matrix_ref in enumerate((mass_ref, stiff_ref)):
        gram = None
        for s in range(sub_dev):
            part = partial_ref[place, s] + jnp.dot(
                matrix_ref[s, :, far], other_ref[s], preferred_element_type=jnp.float32
            )
            part = jnp.where(slot < counts_ref[s], part, 0.0).astype(jnp.bfloat16)
            if place == 1:
                part_ref[s] = part
            term = lax.dot_general(
                mine_ref[s], part, (((0,), (0,)), ((), ())), preferred_element_type=jnp.float32
            )
            gram = term if gram is None else gram + term
        low, high = gram[: width // 2], gram[width // 2 :]
        keep_ref[place] = jnp.where(first, low, high)
        send_ref[place] = jnp.where(first, high, low)


def products(counts, mine, other, stiffness, mass):
    sub_dev, half, width = mine.shape
    vmem = pl.BlockSpec(memory_space=pltpu.VMEM)
    params = pltpu.CompilerParams(vmem_limit_bytes=20 << 20)
    partial = pl.pallas_call(
        own_kernel,
        out_shape=jax.ShapeDtypeStruct((2, sub_dev, half, width), jnp.float32),
        in_specs=[vmem] * 3,
        out_specs=vmem,
        compiler_params=params,
        cost_estimate=pl.CostEstimate(flops=540000000, bytes_accessed=4 << 20, transcendentals=0),
        name="own_half",
    )(mine, stiffness, mass)
    gram = jax.ShapeDtypeStruct((2, width // 2, width), jnp.float32)
    return pl.pallas_call(
        far_kernel,
        out_shape=(jax.ShapeDtypeStruct(mine.shape, jnp.bfloat16), gram, gram),
        in_specs=[pl.BlockSpec(memory_space=pltpu.SMEM)] + [vmem] * 5,
        out_specs=(vmem, vmem, vmem),
        compiler_params=params,
        cost_estimate=pl.CostEstimate(flops=810000000, bytes_accessed=4 << 20, transcendentals=0),
        name="far_half",
    )(counts, partial, mine, other, stiffness, mass)


def eliminate(work_ref, inverse_ref):
    n = work_ref.shape[0]
    row = lax.broadcasted_iota(jnp.int32, (n, n), 0)
    col = lax.broadcasted_iota(jnp.int32, (n, n), 1)
    lane = lax.broadcasted_iota(jnp.int32, (1, n), 1)
    inverse_ref[...] = jnp.where(row == col, 1.0, 0.0)

    def column(k, _):
        pivot_row = work_ref[pl.ds(k, 1), :]
        pivot = jnp.sum(jnp.where(lane == k, pivot_row, 0.0), axis=1, keepdims=True)
        work = work_ref[...]
        inverse = inverse_ref[...]
        below = jnp.sum(jnp.where(col == k, work, 0.0), axis=1, keepdims=True) / pivot
        below = jnp.where(row[:, :1] > k, below, 0.0)
        inverse_row = inverse_ref[pl.ds(k, 1), :]
        work_ref[...] = work - below * pivot_row
        inverse = inverse - below * inverse_row
        inverse_ref[...] = jnp.where(row == k, inverse * lax.rsqrt(pivot), inverse)
        return 0

    lax.fori_loop(0, n, column, 0)


def ritz_kernel(
    scale,
    mine_ref,
    other_ref,
    image_ref,
    extra_ref,
    rotated_hbm,
    projected_hbm,
    gram_ref,
    inverse_ref,
    rotated_ref,
    projected_ref,
    sems,
):
    rows, n = mine_ref.shape[1:]
    me_blk = lax.axis_index("blk")
    own = pl.ds(pl.multiple_of(me_blk * rows, rows), rows)
    far = pl.ds(pl.multiple_of((1 - me_blk) * rows, rows), rows)
    for plane in range(2):
        gram_ref[plane, own, :] = mine_ref[plane]
        gram_ref[plane, far, :] = other_ref[plane]
    row = lax.broadcasted_iota(jnp.int32, (n, n), 0)
    col = lax.broadcasted_iota(jnp.int32, (n, n), 1)
    eye = jnp.where(row == col, 1.0, 0.0)
    weight = jnp.where(row > col, 1.0, 0.5 * eye)
    gram = gram_ref[0]
    gram = 0.5 * (gram + gram.T)
    projected_ref[...] = gram
    on_diag = jnp.where(row == col, gram, 0.0)
    down = lax.rsqrt(jnp.sum(on_diag, axis=1, keepdims=True))
    across = lax.rsqrt(jnp.sum(on_diag, axis=0, keepdims=True))
    rest = jnp.where(row == col, 0.0, gram * down * across)
    gram_ref[0] = rest
    off = -weight * rest
    for _ in range(2):
        left = rest + off + short(off, rest, 0)
        step = weight * (left + off.T + short(left, off, 1))
        off = off - step - short(step, off, 0)
    inverse_ref[...] = off

    def going(state):
        step, size = state
        return jnp.logical_and(step < MAX_STEPS, jnp.logical_not(size < RESIDUAL))

    def correct(state):
        step, _ = state
        off = inverse_ref[...]
        rest = gram_ref[0]
        left = rest + off + long(off, rest, 0)
        error = left + off.T + long(left, off, 1)
        change = weight * error
        inverse_ref[...] = off - change - long(change, off, 0)
        return step + 1, jnp.sum(error * error)

    _, size = lax.while_loop(going, correct, (jnp.int32(0), jnp.float32(1.0)))
    inverse_ref[...] = (eye + inverse_ref[...]) * across

    @pl.when(jnp.logical_not(size < RESIDUAL))
    def _():
        eliminate(projected_ref, inverse_ref)

    inverse = inverse_ref[...]
    rotated_ref[...] = scale * long(image_ref[...] + extra_ref[...], inverse, 1)
    first = pltpu.make_async_copy(rotated_ref, rotated_hbm, sems.at[0])
    first.start()
    projected_ref[...] = long(long(inverse, gram_ref[1], 0), inverse, 1)
    second = pltpu.make_async_copy(projected_ref, projected_hbm, sems.at[1])
    second.start()
    first.wait()
    second.wait()


def ritz(mine, other, image, extra, scale):
    n = mine.shape[2]
    vmem = pl.BlockSpec(memory_space=pltpu.VMEM)
    hbm = pl.BlockSpec(memory_space=pltpu.HBM)
    square = jax.ShapeDtypeStruct((n, n), jnp.float32)
    return pl.pallas_call(
        functools.partial(ritz_kernel, scale),
        out_shape=(square, square),
        in_specs=[vmem] * 4,
        out_specs=(hbm, hbm),
        scratch_shapes=[
            pltpu.VMEM((2, n, n), jnp.float32),
            pltpu.VMEM((n, n), jnp.float32),
            pltpu.VMEM((n, n), jnp.float32),
            pltpu.VMEM((n, n), jnp.float32),
            pltpu.SemaphoreType.DMA((2,)),
        ],
        compiler_params=pltpu.CompilerParams(vmem_limit_bytes=16 << 20),
        name="ritz",
    )(mine, other, image, extra)


def to_pieces(plane):
    rows, wide = plane.shape
    return plane.reshape(rows // 2, 2, 2, wide // 2).transpose(2, 0, 1, 3).reshape(rows, 2, wide // 2)


def from_pieces(pieces):
    rows, _, lanes = pieces.shape
    return pieces.reshape(2, rows // 2, 2, lanes).transpose(1, 2, 0, 3).reshape(rows, 2 * lanes)


def per_device(basis, stiffness, mass, owner_rows, counts):
    n_sub = lax.axis_size("sub")
    me_sub = lax.axis_index("sub")
    me_blk = lax.axis_index("blk")
    rows_dev, width = basis.shape
    sub_dev, half, order = stiffness.shape
    cap = owner_rows.shape[2]
    cap_half = cap // 2
    lanes = width // 2
    table = lax.dynamic_slice_in_dim(owner_rows[0], me_blk * cap_half, cap_half, 1)
    picks = select_rows(table.reshape(-1), rows_dev)

    sent = jnp.dot(picks, basis, preferred_element_type=jnp.float32).astype(jnp.bfloat16)
    received = lax.all_to_all(
        sent.reshape(n_sub, cap_half, width), "sub", split_axis=0, concat_axis=0, tiled=True
    )
    received = lax.optimization_barrier(jnp.roll(received, -me_sub, axis=0))
    mine = received.transpose(1, 0, 2).reshape(sub_dev, half, width)
    slots = me_blk * half + jnp.arange(half, dtype=jnp.int32)
    my_live = (slots[None, :] < counts[:, None])[:, :, None]
    mine = jnp.where(my_live, mine, jnp.zeros((), jnp.bfloat16))
    other = lax.ppermute(mine, "blk", SWAP)
    stiff_part, keep, send = products(counts, mine, other, stiffness, mass)
    grams = keep + lax.ppermute(send, "blk", SWAP)
    terms = [to_pieces(term) for plane in (grams[0], grams[1]) for term in two_terms(plane)]
    outgoing = stiff_part.reshape(cap_half, n_sub, width).transpose(1, 0, 2)
    outgoing = jnp.roll(outgoing, me_sub, axis=0)
    back = lax.all_to_all(
        jnp.concatenate([outgoing, jnp.concatenate(terms, axis=1)], axis=2),
        "sub",
        split_axis=0,
        concat_axis=0,
        tiled=True,
    )
    total = jnp.sum(back[:, :, width:].astype(jnp.float32), axis=0).reshape(2, 2, 2, lanes)
    total = jnp.sum(total, axis=1).reshape(4, lanes)
    spread = lax.all_to_all(
        jnp.broadcast_to(total[None], (n_sub, 4, lanes)),
        "sub",
        split_axis=0,
        concat_axis=0,
        tiled=True,
    )
    mine_grams = jnp.stack([from_pieces(spread[:, :2]), from_pieces(spread[:, 2:])])
    other_grams = lax.ppermute(mine_grams, "blk", SWAP)
    image = jnp.einsum(
        "tr,tc->rc",
        picks,
        back[:, :, :width].reshape(-1, width),
        preferred_element_type=jnp.float32,
    ).reshape(2, rows_dev // 2, width)
    image_k = lax.dynamic_index_in_dim(image, me_blk, 0, keepdims=False)
    extra_k = lax.ppermute(
        lax.dynamic_index_in_dim(image, 1 - me_blk, 0, keepdims=False), "blk", SWAP
    )
    return ritz(mine_grams, other_grams, image_k, extra_k, math.sqrt(rows_dev * n_sub))


def solution(mesh):
    return jax.shard_map(
        per_device,
        mesh=mesh,
        in_specs=(
            P("sub", None),
            P("sub", "blk", None),
            P("sub", "blk", None),
            P("sub", None, None),
            P("sub"),
        ),
        out_specs=(P(("sub", "blk"), None), P()),
        check_vma=False,
    )
```

```python
import functools
import math

import jax
import jax.numpy as jnp
from jax import lax
from jax.experimental.layout import Layout, with_layout_constraint
from jax.experimental import pallas as pl
from jax.experimental.pallas import tpu as pltpu
from jax.sharding import PartitionSpec as P

SWAP = ((0, 1), (1, 0))
MAX_STEPS = 7
RESIDUAL = 1e-6


def select_rows(index, count):
    places = lax.broadcasted_iota(jnp.int32, (index.shape[0], count), 1)
    return (index[:, None] == places).astype(jnp.bfloat16)


def two_terms(value):
    upper = lax.reduce_precision(value, exponent_bits=8, mantissa_bits=7)
    return upper.astype(jnp.bfloat16), (value - upper).astype(jnp.bfloat16)


def short(left, right, side):
    return lax.dot_general(
        left.astype(jnp.bfloat16),
        right.astype(jnp.bfloat16),
        (((1,), (side,)), ((), ())),
        preferred_element_type=jnp.float32,
    )


def long(left, right, side):
    left_top = left.astype(jnp.bfloat16)
    left_rest = left - left_top.astype(jnp.float32)
    right_top = right.astype(jnp.bfloat16)
    right_rest = right - right_top.astype(jnp.float32)
    small = short(left_top, right_rest, side) + short(left_rest, right_top, side)
    return small + short(left_top, right_top, side)


def halves(half):
    me_blk = lax.axis_index("blk")
    own = pl.ds(pl.multiple_of(me_blk * half, half), half)
    far = pl.ds(pl.multiple_of((1 - me_blk) * half, half), half)
    return me_blk, own, far


def own_kernel(mine_ref, stiff_ref, mass_ref, partial_ref, turned_ref):
    sub_dev, half, _ = mine_ref.shape
    _, own, _ = halves(half)
    for s in range(sub_dev):
        turned_ref[s] = mine_ref[s].T
    for place, matrix_ref in enumerate((mass_ref, stiff_ref)):
        for s in range(sub_dev):
            partial_ref[place, s] = jnp.dot(
                matrix_ref[s, :, own], mine_ref[s], preferred_element_type=jnp.float32
            )


def far_kernel(
    counts_ref, partial_ref, turned_ref, other_ref, stiff_ref, mass_ref, part_ref, keep_ref, send_ref
):
    sub_dev, half, width = other_ref.shape
    me_blk, _, far = halves(half)
    first = me_blk == 0
    slot = me_blk * half + lax.broadcasted_iota(jnp.int32, (half, width), 0)
    for place, matrix_ref in enumerate((mass_ref, stiff_ref)):
        gram = None
        for s in range(sub_dev):
            part = partial_ref[place, s] + jnp.dot(
                matrix_ref[s, :, far], other_ref[s], preferred_element_type=jnp.float32
            )
            part = jnp.where(slot < counts_ref[s], part, 0.0).astype(jnp.bfloat16)
            if place == 1:
                part_ref[s] = part
            term = jnp.dot(turned_ref[s], part, preferred_element_type=jnp.float32)
            gram = term if gram is None else gram + term
        low, high = gram[: width // 2], gram[width // 2 :]
        keep_ref[place] = jnp.where(first, low, high)
        send_ref[place] = jnp.where(first, high, low)


def products(counts, mine, other, stiffness, mass):
    sub_dev, half, width = mine.shape
    vmem = pl.BlockSpec(memory_space=pltpu.VMEM)
    params = pltpu.CompilerParams(vmem_limit_bytes=20 << 20)
    partial, turned = pl.pallas_call(
        own_kernel,
        out_shape=(
            jax.ShapeDtypeStruct((2, sub_dev, half, width), jnp.float32),
            jax.ShapeDtypeStruct((sub_dev, width, half), jnp.bfloat16),
        ),
        in_specs=[vmem] * 3,
        out_specs=(vmem, vmem),
        compiler_params=params,
        cost_estimate=pl.CostEstimate(flops=540000000, bytes_accessed=4 << 20, transcendentals=0),
        name="own_half",
    )(mine, stiffness, mass)
    gram = jax.ShapeDtypeStruct((2, width // 2, width), jnp.float32)
    return pl.pallas_call(
        far_kernel,
        out_shape=(jax.ShapeDtypeStruct(mine.shape, jnp.bfloat16), gram, gram),
        in_specs=[pl.BlockSpec(memory_space=pltpu.SMEM)] + [vmem] * 5,
        out_specs=(vmem, vmem, vmem),
        compiler_params=params,
        cost_estimate=pl.CostEstimate(flops=810000000, bytes_accessed=4 << 20, transcendentals=0),
        name="far_half",
    )(counts, partial, turned, other, stiffness, mass)


def eliminate(work_ref, inverse_ref):
    n = work_ref.shape[0]
    row = lax.broadcasted_iota(jnp.int32, (n, n), 0)
    col = lax.broadcasted_iota(jnp.int32, (n, n), 1)
    lane = lax.broadcasted_iota(jnp.int32, (1, n), 1)
    inverse_ref[...] = jnp.where(row == col, 1.0, 0.0)

    def column(k, _):
        pivot_row = work_ref[pl.ds(k, 1), :]
        pivot = jnp.sum(jnp.where(lane == k, pivot_row, 0.0), axis=1, keepdims=True)
        work = work_ref[...]
        inverse = inverse_ref[...]
        below = jnp.sum(jnp.where(col == k, work, 0.0), axis=1, keepdims=True) / pivot
        below = jnp.where(row[:, :1] > k, below, 0.0)
        inverse_row = inverse_ref[pl.ds(k, 1), :]
        work_ref[...] = work - below * pivot_row
        inverse = inverse - below * inverse_row
        inverse_ref[...] = jnp.where(row == k, inverse * lax.rsqrt(pivot), inverse)
        return 0

    lax.fori_loop(0, n, column, 0)


def ritz_kernel(
    scale,
    mine_ref,
    other_ref,
    image_ref,
    extra_ref,
    rotated_hbm,
    projected_hbm,
    gram_ref,
    inverse_ref,
    rotated_ref,
    projected_ref,
    sems,
):
    rows, n = mine_ref.shape[1:]
    me_blk = lax.axis_index("blk")
    own = pl.ds(pl.multiple_of(me_blk * rows, rows), rows)
    far = pl.ds(pl.multiple_of((1 - me_blk) * rows, rows), rows)
    for plane in range(2):
        gram_ref[plane, own, :] = mine_ref[plane]
        gram_ref[plane, far, :] = other_ref[plane]
    row = lax.broadcasted_iota(jnp.int32, (n, n), 0)
    col = lax.broadcasted_iota(jnp.int32, (n, n), 1)
    eye = jnp.where(row == col, 1.0, 0.0)
    weight = jnp.where(row > col, 1.0, 0.5 * eye)
    gram = gram_ref[0]
    gram = 0.5 * (gram + gram.T)
    projected_ref[...] = gram
    on_diag = jnp.where(row == col, gram, 0.0)
    down = lax.rsqrt(jnp.sum(on_diag, axis=1, keepdims=True))
    across = lax.rsqrt(jnp.sum(on_diag, axis=0, keepdims=True))
    rest = jnp.where(row == col, 0.0, gram * down * across)
    gram_ref[0] = rest
    off = -weight * rest
    for _ in range(2):
        left = rest + off + short(off, rest, 0)
        step = weight * (left + off.T + short(left, off, 1))
        off = off - step - short(step, off, 0)
    inverse_ref[...] = off

    def going(state):
        step, size = state
        return jnp.logical_and(step < MAX_STEPS, jnp.logical_not(size < RESIDUAL))

    def correct(state):
        step, _ = state
        off = inverse_ref[...]
        rest = gram_ref[0]
        left = rest + off + long(off, rest, 0)
        error = left + off.T + long(left, off, 1)
        change = weight * error
        inverse_ref[...] = off - change - long(change, off, 0)
        return step + 1, jnp.sum(error * error)

    _, size = lax.while_loop(going, correct, (jnp.int32(0), jnp.float32(1.0)))
    inverse_ref[...] = (eye + inverse_ref[...]) * across

    @pl.when(jnp.logical_not(size < RESIDUAL))
    def _():
        eliminate(projected_ref, inverse_ref)

    inverse = inverse_ref[...]
    rotated_ref[...] = scale * long(image_ref[...] + extra_ref[...], inverse, 1)
    first = pltpu.make_async_copy(rotated_ref, rotated_hbm, sems.at[0])
    first.start()
    projected_ref[...] = long(long(inverse, gram_ref[1], 0), inverse, 1)
    second = pltpu.make_async_copy(projected_ref, projected_hbm, sems.at[1])
    second.start()
    first.wait()
    second.wait()


def ritz(mine, other, image, extra, scale):
    n = mine.shape[2]
    vmem = pl.BlockSpec(memory_space=pltpu.VMEM)
    hbm = pl.BlockSpec(memory_space=pltpu.HBM)
    square = jax.ShapeDtypeStruct((n, n), jnp.float32)
    return pl.pallas_call(
        functools.partial(ritz_kernel, scale),
        out_shape=(square, square),
        in_specs=[vmem] * 4,
        out_specs=(hbm, hbm),
        scratch_shapes=[
            pltpu.VMEM((2, n, n), jnp.float32),
            pltpu.VMEM((n, n), jnp.float32),
            pltpu.VMEM((n, n), jnp.float32),
            pltpu.VMEM((n, n), jnp.float32),
            pltpu.SemaphoreType.DMA((2,)),
        ],
        compiler_params=pltpu.CompilerParams(vmem_limit_bytes=16 << 20),
        name="ritz",
    )(mine, other, image, extra)


def to_pieces(planes):
    n, rows, wide = planes.shape
    pieces = planes.reshape(n, 2, rows // 2, 2, wide // 2).transpose(3, 2, 0, 1, 4)
    return pieces.reshape(rows, 2 * n, wide // 2)


def from_pieces(pieces):
    rows, double, lanes = pieces.shape
    planes = pieces.reshape(2, rows // 2, double // 2, 2, lanes).transpose(2, 3, 1, 0, 4)
    return planes.reshape(double // 2, rows, 2 * lanes)


def per_device(basis, stiffness, mass, owner_rows, counts):
    n_sub = lax.axis_size("sub")
    me_sub = lax.axis_index("sub")
    me_blk = lax.axis_index("blk")
    rows_dev, width = basis.shape
    sub_dev, half, order = stiffness.shape
    cap = owner_rows.shape[2]
    cap_half = cap // 2
    lanes = width // 2
    table = lax.dynamic_slice_in_dim(owner_rows[0], me_blk * cap_half, cap_half, 1)
    picks = select_rows(table.reshape(-1), rows_dev)

    sent = jnp.dot(picks, basis, preferred_element_type=jnp.float32).astype(jnp.bfloat16)
    received = lax.all_to_all(
        sent.reshape(n_sub, cap_half, width), "sub", split_axis=0, concat_axis=0, tiled=True
    )
    received = with_layout_constraint(received.transpose(1, 0, 2), Layout((0, 1, 2)))
    mine = jnp.roll(received, -me_sub, axis=1).reshape(sub_dev, half, width)
    slots = me_blk * half + jnp.arange(half, dtype=jnp.int32)
    my_live = (slots[None, :] < counts[:, None])[:, :, None]
    mine = jnp.where(my_live, mine, jnp.zeros((), jnp.bfloat16))
    other = lax.ppermute(mine, "blk", SWAP)
    stiff_part, keep, send = products(counts, mine, other, stiffness, mass)
    grams = keep + lax.ppermute(send, "blk", SWAP)
    terms = to_pieces(jnp.concatenate(two_terms(grams)))
    outgoing = stiff_part.reshape(cap_half, n_sub, width).transpose(1, 0, 2)
    outgoing = jnp.roll(outgoing, me_sub, axis=0)
    back = lax.all_to_all(
        jnp.concatenate([outgoing, terms], axis=2),
        "sub",
        split_axis=0,
        concat_axis=0,
        tiled=True,
    )
    total = jnp.sum(back[:, :, width:].astype(jnp.float32), axis=0)
    total = total[:4] + total[4:]
    spread = lax.all_to_all(
        jnp.broadcast_to(total[None], (n_sub, 4, lanes)),
        "sub",
        split_axis=0,
        concat_axis=0,
        tiled=True,
    )
    mine_grams = from_pieces(spread)
    other_grams = lax.ppermute(mine_grams, "blk", SWAP)
    image = jnp.einsum(
        "tr,tc->rc",
        picks,
        back[:, :, :width].reshape(-1, width),
        preferred_element_type=jnp.float32,
    ).reshape(2, rows_dev // 2, width)
    image_k = lax.dynamic_index_in_dim(image, me_blk, 0, keepdims=False)
    extra_k = lax.ppermute(
        lax.dynamic_index_in_dim(image, 1 - me_blk, 0, keepdims=False), "blk", SWAP
    )
    return ritz(mine_grams, other_grams, image_k, extra_k, math.sqrt(rows_dev * n_sub))


def solution(mesh):
    return jax.shard_map(
        per_device,
        mesh=mesh,
        in_specs=(
            P("sub", None),
            P("sub", "blk", None),
            P("sub", "blk", None),
            P("sub", None, None),
            P("sub"),
        ),
        out_specs=(P(("sub", "blk"), None), P()),
        check_vma=False,
    )
```

```python
import functools
import math

import jax
import jax.numpy as jnp
from jax import lax
from jax.experimental.layout import Layout, with_layout_constraint
from jax.experimental import pallas as pl
from jax.experimental.pallas import tpu as pltpu
from jax.sharding import PartitionSpec as P

SWAP = ((0, 1), (1, 0))
MAX_STEPS = 7
RESIDUAL = 1e-6


def select_rows(index, count):
    places = lax.broadcasted_iota(jnp.int32, (index.shape[0], count), 1)
    return (index[:, None] == places).astype(jnp.bfloat16)


def two_terms(value):
    upper = lax.reduce_precision(value, exponent_bits=8, mantissa_bits=7)
    return upper.astype(jnp.bfloat16), (value - upper).astype(jnp.bfloat16)


def short(left, right, side):
    return lax.dot_general(
        left.astype(jnp.bfloat16),
        right.astype(jnp.bfloat16),
        (((1,), (side,)), ((), ())),
        preferred_element_type=jnp.float32,
    )


def long(left, right, side):
    left_top = left.astype(jnp.bfloat16)
    left_rest = left - left_top.astype(jnp.float32)
    right_top = right.astype(jnp.bfloat16)
    right_rest = right - right_top.astype(jnp.float32)
    small = short(left_top, right_rest, side) + short(left_rest, right_top, side)
    return small + short(left_top, right_top, side)


def halves(half):
    me_blk = lax.axis_index("blk")
    own = pl.ds(pl.multiple_of(me_blk * half, half), half)
    far = pl.ds(pl.multiple_of((1 - me_blk) * half, half), half)
    return me_blk, own, far


def own_kernel(mine_ref, matrix_ref, partial_ref, turned_ref=None):
    sub_dev, half, _ = mine_ref.shape
    _, own, _ = halves(half)
    for s in range(sub_dev):
        partial_ref[s] = jnp.dot(
            matrix_ref[s, :, own], mine_ref[s], preferred_element_type=jnp.float32
        )
        if turned_ref is not None:
            turned_ref[:, s * half : (s + 1) * half] = mine_ref[s].T


def far_kernel(
    counts_ref,
    stiff_own_ref,
    mass_own_ref,
    turned_ref,
    other_ref,
    stiff_ref,
    mass_ref,
    part_ref,
    keep_ref,
    send_ref,
    mass_part_ref,
):
    sub_dev, half, width = other_ref.shape
    me_blk, _, far = halves(half)
    first = me_blk == 0
    slot = me_blk * half + lax.broadcasted_iota(jnp.int32, (half, 1), 0)
    for s in range(sub_dev):
        part = mass_own_ref[s] + jnp.dot(
            mass_ref[s, :, far], other_ref[s], preferred_element_type=jnp.float32
        )
        mass_part_ref[s] = jnp.where(slot < counts_ref[s], part, 0.0).astype(jnp.bfloat16)
    for s in range(sub_dev):
        part = stiff_own_ref[s] + jnp.dot(
            stiff_ref[s, :, far], other_ref[s], preferred_element_type=jnp.float32
        )
        part_ref[s] = jnp.where(slot < counts_ref[s], part, 0.0).astype(jnp.bfloat16)
    for place, parts_ref in enumerate((mass_part_ref, part_ref)):
        parts = parts_ref[...].reshape(sub_dev * half, width)
        gram = jnp.dot(turned_ref[...], parts, preferred_element_type=jnp.float32)
        low, high = gram[: width // 2], gram[width // 2 :]
        keep_ref[place] = jnp.where(first, low, high)
        send_ref[place] = jnp.where(first, high, low)


def products(counts, mine, other, stiffness, mass):
    sub_dev, half, width = mine.shape
    vmem = pl.BlockSpec(memory_space=pltpu.VMEM)
    params = pltpu.CompilerParams(vmem_limit_bytes=20 << 20)
    partial = jax.ShapeDtypeStruct((sub_dev, half, width), jnp.float32)
    cost = pl.CostEstimate(flops=270000000, bytes_accessed=2 << 20, transcendentals=0)
    stiff_own, turned = pl.pallas_call(
        own_kernel,
        out_shape=(partial, jax.ShapeDtypeStruct((width, sub_dev * half), jnp.bfloat16)),
        in_specs=[vmem] * 2,
        out_specs=(vmem, vmem),
        compiler_params=params,
        cost_estimate=cost,
        name="own_stiff",
    )(mine, stiffness)
    mass_own = pl.pallas_call(
        own_kernel,
        out_shape=partial,
        in_specs=[vmem] * 2,
        out_specs=vmem,
        compiler_params=params,
        cost_estimate=cost,
        name="own_mass",
    )(mine, mass)
    gram = jax.ShapeDtypeStruct((2, width // 2, width), jnp.float32)
    return pl.pallas_call(
        far_kernel,
        out_shape=(jax.ShapeDtypeStruct(mine.shape, jnp.bfloat16), gram, gram),
        in_specs=[pl.BlockSpec(memory_space=pltpu.SMEM)] + [vmem] * 6,
        out_specs=(vmem, vmem, vmem),
        scratch_shapes=[pltpu.VMEM((sub_dev, half, width), jnp.bfloat16)],
        compiler_params=params,
        cost_estimate=pl.CostEstimate(flops=810000000, bytes_accessed=4 << 20, transcendentals=0),
        name="far_half",
    )(counts, stiff_own, mass_own, turned, other, stiffness, mass)


def eliminate(work_ref, inverse_ref):
    n = work_ref.shape[0]
    row = lax.broadcasted_iota(jnp.int32, (n, n), 0)
    col = lax.broadcasted_iota(jnp.int32, (n, n), 1)
    lane = lax.broadcasted_iota(jnp.int32, (1, n), 1)
    inverse_ref[...] = jnp.where(row == col, 1.0, 0.0)

    def column(k, _):
        pivot_row = work_ref[pl.ds(k, 1), :]
        pivot = jnp.sum(jnp.where(lane == k, pivot_row, 0.0), axis=1, keepdims=True)
        work = work_ref[...]
        inverse = inverse_ref[...]
        below = jnp.sum(jnp.where(col == k, work, 0.0), axis=1, keepdims=True) / pivot
        below = jnp.where(row[:, :1] > k, below, 0.0)
        inverse_row = inverse_ref[pl.ds(k, 1), :]
        work_ref[...] = work - below * pivot_row
        inverse = inverse - below * inverse_row
        inverse_ref[...] = jnp.where(row == k, inverse * lax.rsqrt(pivot), inverse)
        return 0

    lax.fori_loop(0, n, column, 0)


def ritz_kernel(
    scale,
    mine_ref,
    other_ref,
    image_ref,
    extra_ref,
    rotated_hbm,
    projected_hbm,
    gram_ref,
    inverse_ref,
    rotated_ref,
    projected_ref,
    sems,
):
    rows, n = mine_ref.shape[1:]
    me_blk = lax.axis_index("blk")
    own = pl.ds(pl.multiple_of(me_blk * rows, rows), rows)
    far = pl.ds(pl.multiple_of((1 - me_blk) * rows, rows), rows)
    for plane in range(2):
        gram_ref[plane, own, :] = mine_ref[plane]
        gram_ref[plane, far, :] = other_ref[plane]
    row = lax.broadcasted_iota(jnp.int32, (n, n), 0)
    col = lax.broadcasted_iota(jnp.int32, (n, n), 1)
    eye = jnp.where(row == col, 1.0, 0.0)
    weight = jnp.where(row > col, 1.0, 0.5 * eye)
    gram = gram_ref[0]
    gram = 0.5 * (gram + gram.T)
    projected_ref[...] = gram
    on_diag = jnp.where(row == col, gram, 0.0)
    down = lax.rsqrt(jnp.sum(on_diag, axis=1, keepdims=True))
    across = lax.rsqrt(jnp.sum(on_diag, axis=0, keepdims=True))
    rest = jnp.where(row == col, 0.0, gram * down * across)
    gram_ref[0] = rest
    off = -weight * rest
    for _ in range(2):
        left = rest + off + short(off, rest, 0)
        step = weight * (left + off.T + short(left, off, 1))
        off = off - step - short(step, off, 0)
    inverse_ref[...] = off

    def going(state):
        step, size = state
        return jnp.logical_and(step < MAX_STEPS, jnp.logical_not(size < RESIDUAL))

    def correct(state):
        step, _ = state
        off = inverse_ref[...]
        rest = gram_ref[0]
        left = rest + off + long(off, rest, 0)
        error = left + off.T + long(left, off, 1)
        change = weight * error
        inverse_ref[...] = off - change - short(change, off, 0)
        return step + 1, jnp.sum(error * error)

    _, size = lax.while_loop(going, correct, (jnp.int32(0), jnp.float32(1.0)))
    inverse_ref[...] = (eye + inverse_ref[...]) * across

    @pl.when(jnp.logical_not(size < RESIDUAL))
    def _():
        eliminate(projected_ref, inverse_ref)

    inverse = inverse_ref[...]
    rotated_ref[...] = scale * long(image_ref[...] + extra_ref[...], inverse, 1)
    first = pltpu.make_async_copy(rotated_ref, rotated_hbm, sems.at[0])
    first.start()
    projected_ref[...] = long(long(inverse, gram_ref[1], 0), inverse, 1)
    second = pltpu.make_async_copy(projected_ref, projected_hbm, sems.at[1])
    second.start()
    first.wait()
    second.wait()


def ritz(mine, other, image, extra, scale):
    n = mine.shape[2]
    vmem = pl.BlockSpec(memory_space=pltpu.VMEM)
    hbm = pl.BlockSpec(memory_space=pltpu.HBM)
    square = jax.ShapeDtypeStruct((n, n), jnp.float32)
    return pl.pallas_call(
        functools.partial(ritz_kernel, scale),
        out_shape=(square, square),
        in_specs=[vmem] * 4,
        out_specs=(hbm, hbm),
        scratch_shapes=[
            pltpu.VMEM((2, n, n), jnp.float32),
            pltpu.VMEM((n, n), jnp.float32),
            pltpu.VMEM((n, n), jnp.float32),
            pltpu.VMEM((n, n), jnp.float32),
            pltpu.SemaphoreType.DMA((2,)),
        ],
        compiler_params=pltpu.CompilerParams(vmem_limit_bytes=16 << 20),
        name="ritz",
    )(mine, other, image, extra)


def to_pieces(planes):
    n, rows, wide = planes.shape
    pieces = planes.reshape(n, 2, rows // 2, 2, wide // 2).transpose(3, 2, 0, 1, 4)
    return pieces.reshape(rows, 2 * n, wide // 2)


def from_pieces(pieces):
    rows, double, lanes = pieces.shape
    planes = pieces.reshape(2, rows // 2, double // 2, 2, lanes).transpose(2, 3, 1, 0, 4)
    return planes.reshape(double // 2, rows, 2 * lanes)


def per_device(basis, stiffness, mass, owner_rows, counts):
    n_sub = lax.axis_size("sub")
    me_sub = lax.axis_index("sub")
    me_blk = lax.axis_index("blk")
    rows_dev, width = basis.shape
    sub_dev, half, order = stiffness.shape
    cap = owner_rows.shape[2]
    cap_half = cap // 2
    lanes = width // 2
    table = lax.dynamic_slice_in_dim(owner_rows[0], me_blk * cap_half, cap_half, 1)
    picks = select_rows(table.reshape(-1), rows_dev)

    sent = jnp.dot(picks, basis, preferred_element_type=jnp.float32).astype(jnp.bfloat16)
    received = lax.all_to_all(
        sent.reshape(n_sub, cap_half, width), "sub", split_axis=0, concat_axis=0, tiled=True
    )
    received = with_layout_constraint(received.transpose(1, 0, 2), Layout((0, 1, 2)))
    mine = jnp.roll(received, -me_sub, axis=1).reshape(sub_dev, half, width)
    slots = me_blk * half + jnp.arange(half, dtype=jnp.int32)
    my_live = (slots[None, :] < counts[:, None])[:, :, None]
    mine = jnp.where(my_live, mine, jnp.zeros((), jnp.bfloat16))
    other = lax.ppermute(mine, "blk", SWAP)
    stiff_part, keep, send = products(counts, mine, other, stiffness, mass)
    grams = keep + lax.ppermute(send, "blk", SWAP)
    terms = to_pieces(jnp.concatenate(two_terms(grams)))
    outgoing = stiff_part.reshape(cap_half, n_sub, width).transpose(1, 0, 2)
    outgoing = jnp.roll(outgoing, me_sub, axis=0)
    back = lax.all_to_all(
        jnp.concatenate([outgoing, terms], axis=2),
        "sub",
        split_axis=0,
        concat_axis=0,
        tiled=True,
    )
    total = jnp.sum(back[:, :, width:].astype(jnp.float32), axis=0)
    total = total[:4] + total[4:]
    spread = lax.all_to_all(
        jnp.broadcast_to(total[None], (n_sub, 4, lanes)),
        "sub",
        split_axis=0,
        concat_axis=0,
        tiled=True,
    )
    mine_grams = from_pieces(spread)
    other_grams = lax.ppermute(mine_grams, "blk", SWAP)
    image = jnp.einsum(
        "tr,tc->rc",
        picks,
        back[:, :, :width].reshape(-1, width),
        preferred_element_type=jnp.float32,
    ).reshape(2, rows_dev // 2, width)
    image_k = lax.dynamic_index_in_dim(image, me_blk, 0, keepdims=False)
    extra_k = lax.ppermute(
        lax.dynamic_index_in_dim(image, 1 - me_blk, 0, keepdims=False), "blk", SWAP
    )
    return ritz(mine_grams, other_grams, image_k, extra_k, math.sqrt(rows_dev * n_sub))


def solution(mesh):
    return jax.shard_map(
        per_device,
        mesh=mesh,
        in_specs=(
            P("sub", None),
            P("sub", "blk", None),
            P("sub", "blk", None),
            P("sub", None, None),
            P("sub"),
        ),
        out_specs=(P(("sub", "blk"), None), P()),
        check_vma=False,
    )
```

```python
import functools
import math

import jax
import jax.numpy as jnp
from jax import lax
from jax.experimental.layout import Layout, with_layout_constraint
from jax.experimental import pallas as pl
from jax.experimental.pallas import tpu as pltpu
from jax.sharding import PartitionSpec as P

SWAP = ((0, 1), (1, 0))
MAX_STEPS = 7
RESIDUAL = 1e-6


def select_rows(index, count):
    places = lax.broadcasted_iota(jnp.int32, (index.shape[0], count), 1)
    return (index[:, None] == places).astype(jnp.bfloat16)


def two_terms(value):
    upper = lax.reduce_precision(value, exponent_bits=8, mantissa_bits=7)
    return upper.astype(jnp.bfloat16), (value - upper).astype(jnp.bfloat16)


def short(left, right, side):
    return lax.dot_general(
        left.astype(jnp.bfloat16),
        right.astype(jnp.bfloat16),
        (((1,), (side,)), ((), ())),
        preferred_element_type=jnp.float32,
    )


def long(left, right, side):
    left_top = left.astype(jnp.bfloat16)
    left_rest = left - left_top.astype(jnp.float32)
    right_top = right.astype(jnp.bfloat16)
    right_rest = right - right_top.astype(jnp.float32)
    small = short(left_top, right_rest, side) + short(left_rest, right_top, side)
    return small + short(left_top, right_top, side)


def halves(half):
    me_blk = lax.axis_index("blk")
    own = pl.ds(pl.multiple_of(me_blk * half, half), half)
    far = pl.ds(pl.multiple_of((1 - me_blk) * half, half), half)
    return me_blk, own, far


def own_kernel(mine_ref, matrix_ref, partial_ref, turned_ref=None):
    sub_dev, half, _ = mine_ref.shape
    _, own, _ = halves(half)
    for s in range(sub_dev):
        partial_ref[s] = jnp.dot(
            matrix_ref[s, :, own], mine_ref[s], preferred_element_type=jnp.float32
        )
        if turned_ref is not None:
            turned_ref[:, s * half : (s + 1) * half] = mine_ref[s].T


def far_kernel(
    counts_ref,
    stiff_own_ref,
    mass_own_ref,
    turned_ref,
    other_ref,
    stiff_ref,
    mass_ref,
    part_ref,
    keep_ref,
    send_ref,
    mass_part_ref,
):
    sub_dev, half, width = other_ref.shape
    me_blk, _, far = halves(half)
    first = me_blk == 0
    slot = me_blk * half + lax.broadcasted_iota(jnp.int32, (half, 1), 0)
    for s in range(sub_dev):
        part = mass_own_ref[s] + jnp.dot(
            mass_ref[s, :, far], other_ref[s], preferred_element_type=jnp.float32
        )
        mass_part_ref[s] = jnp.where(slot < counts_ref[s], part, 0.0).astype(jnp.bfloat16)
    for s in range(sub_dev):
        part = stiff_own_ref[s] + jnp.dot(
            stiff_ref[s, :, far], other_ref[s], preferred_element_type=jnp.float32
        )
        part_ref[s] = jnp.where(slot < counts_ref[s], part, 0.0).astype(jnp.bfloat16)
    for place, parts_ref in enumerate((mass_part_ref, part_ref)):
        parts = parts_ref[...].reshape(sub_dev * half, width)
        gram = jnp.dot(turned_ref[...], parts, preferred_element_type=jnp.float32)
        low, high = gram[: width // 2], gram[width // 2 :]
        keep_ref[place] = jnp.where(first, low, high)
        send_ref[place] = jnp.where(first, high, low)


def products(counts, mine, other, stiffness, mass):
    sub_dev, half, width = mine.shape
    vmem = pl.BlockSpec(memory_space=pltpu.VMEM)
    params = pltpu.CompilerParams(vmem_limit_bytes=20 << 20)
    partial = jax.ShapeDtypeStruct((sub_dev, half, width), jnp.float32)
    cost = pl.CostEstimate(flops=270000000, bytes_accessed=2 << 20, transcendentals=0)
    stiff_own, turned = pl.pallas_call(
        own_kernel,
        out_shape=(partial, jax.ShapeDtypeStruct((width, sub_dev * half), jnp.bfloat16)),
        in_specs=[vmem] * 2,
        out_specs=(vmem, vmem),
        compiler_params=params,
        cost_estimate=cost,
        name="own_stiff",
    )(mine, stiffness)
    mass_own = pl.pallas_call(
        own_kernel,
        out_shape=partial,
        in_specs=[vmem] * 2,
        out_specs=vmem,
        compiler_params=params,
        cost_estimate=cost,
        name="own_mass",
    )(mine, mass)
    gram = jax.ShapeDtypeStruct((2, width // 2, width), jnp.float32)
    return pl.pallas_call(
        far_kernel,
        out_shape=(jax.ShapeDtypeStruct(mine.shape, jnp.bfloat16), gram, gram),
        in_specs=[pl.BlockSpec(memory_space=pltpu.SMEM)] + [vmem] * 6,
        out_specs=(vmem, vmem, vmem),
        scratch_shapes=[pltpu.VMEM((sub_dev, half, width), jnp.bfloat16)],
        compiler_params=params,
        cost_estimate=pl.CostEstimate(flops=810000000, bytes_accessed=4 << 20, transcendentals=0),
        name="far_half",
    )(counts, stiff_own, mass_own, turned, other, stiffness, mass)


def eliminate(work_ref, inverse_ref):
    n = work_ref.shape[0]
    row = lax.broadcasted_iota(jnp.int32, (n, n), 0)
    col = lax.broadcasted_iota(jnp.int32, (n, n), 1)
    lane = lax.broadcasted_iota(jnp.int32, (1, n), 1)
    inverse_ref[...] = jnp.where(row == col, 1.0, 0.0)

    def column(k, _):
        pivot_row = work_ref[pl.ds(k, 1), :]
        pivot = jnp.sum(jnp.where(lane == k, pivot_row, 0.0), axis=1, keepdims=True)
        work = work_ref[...]
        inverse = inverse_ref[...]
        below = jnp.sum(jnp.where(col == k, work, 0.0), axis=1, keepdims=True) / pivot
        below = jnp.where(row[:, :1] > k, below, 0.0)
        inverse_row = inverse_ref[pl.ds(k, 1), :]
        work_ref[...] = work - below * pivot_row
        inverse = inverse - below * inverse_row
        inverse_ref[...] = jnp.where(row == k, inverse * lax.rsqrt(pivot), inverse)
        return 0

    lax.fori_loop(0, n, column, 0)


def ritz_kernel(
    scale,
    mine_ref,
    other_ref,
    image_ref,
    extra_ref,
    rotated_hbm,
    projected_hbm,
    gram_ref,
    inverse_ref,
    rotated_ref,
    projected_ref,
    sems,
):
    rows, n = mine_ref.shape[1:]
    me_blk = lax.axis_index("blk")
    own = pl.ds(pl.multiple_of(me_blk * rows, rows), rows)
    far = pl.ds(pl.multiple_of((1 - me_blk) * rows, rows), rows)
    for plane in range(2):
        gram_ref[plane, own, :] = mine_ref[plane]
        gram_ref[plane, far, :] = other_ref[plane]
    row = lax.broadcasted_iota(jnp.int32, (n, n), 0)
    col = lax.broadcasted_iota(jnp.int32, (n, n), 1)
    eye = jnp.where(row == col, 1.0, 0.0)
    weight = jnp.where(row > col, 1.0, 0.5 * eye)
    gram = gram_ref[0]
    gram = 0.5 * (gram + gram.T)
    projected_ref[...] = gram
    on_diag = jnp.where(row == col, gram, 0.0)
    down = lax.rsqrt(jnp.sum(on_diag, axis=1, keepdims=True))
    across = lax.rsqrt(jnp.sum(on_diag, axis=0, keepdims=True))
    rest = jnp.where(row == col, 0.0, gram * down * across)
    gram_ref[0] = rest
    off = -weight * rest
    for _ in range(2):
        left = rest + off + short(off, rest, 0)
        step = weight * (left + off.T + short(left, off, 1))
        off = off - step - short(step, off, 0)
    inverse_ref[...] = off

    def going(state):
        step, size = state
        return jnp.logical_and(step < MAX_STEPS, jnp.logical_not(size < RESIDUAL))

    def correct(state):
        step, _ = state
        off = inverse_ref[...]
        rest = gram_ref[0]
        left = rest + off + long(off, rest, 0)
        error = left + off.T + long(left, off, 1)
        change = weight * error
        inverse_ref[...] = off - change - short(change, off, 0)
        return step + 1, jnp.sum(error * error)

    _, size = lax.while_loop(going, correct, (jnp.int32(0), jnp.float32(1.0)))
    inverse_ref[...] = (eye + inverse_ref[...]) * across

    @pl.when(jnp.logical_not(size < RESIDUAL))
    def _():
        eliminate(projected_ref, inverse_ref)

    inverse = inverse_ref[...]
    rotated_ref[...] = scale * long(image_ref[...] + extra_ref[...], inverse, 1)
    first = pltpu.make_async_copy(rotated_ref, rotated_hbm, sems.at[0])
    first.start()
    projected_ref[...] = long(long(inverse, gram_ref[1], 0), inverse, 1)
    second = pltpu.make_async_copy(projected_ref, projected_hbm, sems.at[1])
    second.start()
    first.wait()
    second.wait()


def ritz(mine, other, image, extra, scale):
    n = mine.shape[2]
    vmem = pl.BlockSpec(memory_space=pltpu.VMEM)
    hbm = pl.BlockSpec(memory_space=pltpu.HBM)
    square = jax.ShapeDtypeStruct((n, n), jnp.float32)
    return pl.pallas_call(
        functools.partial(ritz_kernel, scale),
        out_shape=(square, square),
        in_specs=[vmem] * 4,
        out_specs=(hbm, hbm),
        scratch_shapes=[
            pltpu.VMEM((2, n, n), jnp.float32),
            pltpu.VMEM((n, n), jnp.float32),
            pltpu.VMEM((n, n), jnp.float32),
            pltpu.VMEM((n, n), jnp.float32),
            pltpu.SemaphoreType.DMA((2,)),
        ],
        compiler_params=pltpu.CompilerParams(vmem_limit_bytes=16 << 20),
        name="ritz",
    )(mine, other, image, extra)


def to_pieces(planes):
    n, rows, wide = planes.shape
    pieces = planes.reshape(n, 2, rows // 2, 2, wide // 2).transpose(3, 2, 0, 1, 4)
    return pieces.reshape(rows, 2 * n, wide // 2)


def from_pieces(pieces):
    rows, double, lanes = pieces.shape
    planes = pieces.reshape(2, rows // 2, double // 2, 2, lanes).transpose(2, 3, 1, 0, 4)
    return planes.reshape(double // 2, rows, 2 * lanes)


def per_device(basis, stiffness, mass, owner_rows, counts):
    n_sub = lax.axis_size("sub")
    me_sub = lax.axis_index("sub")
    me_blk = lax.axis_index("blk")
    rows_dev, width = basis.shape
    sub_dev, half, order = stiffness.shape
    cap = owner_rows.shape[2]
    cap_half = cap // 2
    lanes = width // 2
    table = lax.dynamic_slice_in_dim(owner_rows[0], me_blk * cap_half, cap_half, 1)
    picks = select_rows(table.reshape(-1), rows_dev)

    sent = jnp.dot(picks, basis, preferred_element_type=jnp.float32).astype(jnp.bfloat16)
    sent, me_sub, me_blk = lax.optimization_barrier((sent, me_sub, me_blk))
    received = lax.all_to_all(
        sent.reshape(n_sub, cap_half, width), "sub", split_axis=0, concat_axis=0, tiled=True
    )
    received, counts, me_sub, me_blk = lax.optimization_barrier((received, counts, me_sub, me_blk))
    received = with_layout_constraint(received.transpose(1, 0, 2), Layout((0, 1, 2)))
    mine = jnp.roll(received, -me_sub, axis=1).reshape(sub_dev, half, width)
    slots = jnp.arange(half, dtype=jnp.int32)
    my_live = (slots[None, :] < (counts - me_blk * half)[:, None])[:, :, None]
    mine = jnp.where(my_live, mine, jnp.zeros((), jnp.bfloat16))
    other = lax.ppermute(mine, "blk", SWAP)
    stiff_part, keep, send = products(counts, mine, other, stiffness, mass)
    grams = keep + lax.ppermute(send, "blk", SWAP)
    terms = to_pieces(jnp.concatenate(two_terms(grams)))
    outgoing = stiff_part.reshape(cap_half, n_sub, width).transpose(1, 0, 2)
    outgoing = jnp.roll(outgoing, me_sub, axis=0)
    back = lax.all_to_all(
        jnp.concatenate([outgoing, terms], axis=2),
        "sub",
        split_axis=0,
        concat_axis=0,
        tiled=True,
    )
    total = jnp.sum(back[:, :, width:].astype(jnp.float32), axis=0)
    total = total[:4] + total[4:]
    spread = lax.all_to_all(
        jnp.broadcast_to(total[None], (n_sub, 4, lanes)),
        "sub",
        split_axis=0,
        concat_axis=0,
        tiled=True,
    )
    mine_grams = from_pieces(spread)
    other_grams = lax.ppermute(mine_grams, "blk", SWAP)
    image = jnp.einsum(
        "tr,tc->rc",
        picks,
        back[:, :, :width].reshape(-1, width),
        preferred_element_type=jnp.float32,
    ).reshape(2, rows_dev // 2, width)
    image_k = lax.dynamic_index_in_dim(image, me_blk, 0, keepdims=False)
    extra_k = lax.ppermute(
        lax.dynamic_index_in_dim(image, 1 - me_blk, 0, keepdims=False), "blk", SWAP
    )
    return ritz(mine_grams, other_grams, image_k, extra_k, math.sqrt(rows_dev * n_sub))


def solution(mesh):
    return jax.shard_map(
        per_device,
        mesh=mesh,
        in_specs=(
            P("sub", None),
            P("sub", "blk", None),
            P("sub", "blk", None),
            P("sub", None, None),
            P("sub"),
        ),
        out_specs=(P(("sub", "blk"), None), P()),
        check_vma=False,
    )
```

```python
import functools
import math

import jax
import jax.numpy as jnp
from jax import lax
from jax.experimental.layout import Layout, with_layout_constraint
from jax.experimental import pallas as pl
from jax.experimental.pallas import tpu as pltpu
from jax.sharding import PartitionSpec as P

SWAP = ((0, 1), (1, 0))
MAX_STEPS = 7
RESIDUAL = 1e-6


def select_rows(index, count):
    places = lax.broadcasted_iota(jnp.int32, (index.shape[0], count), 1)
    return (index[:, None] == places).astype(jnp.bfloat16)


def two_terms(value):
    upper = lax.reduce_precision(value, exponent_bits=8, mantissa_bits=7)
    return upper.astype(jnp.bfloat16), (value - upper).astype(jnp.bfloat16)


def short(left, right, side):
    return lax.dot_general(
        left.astype(jnp.bfloat16),
        right.astype(jnp.bfloat16),
        (((1,), (side,)), ((), ())),
        preferred_element_type=jnp.float32,
    )


def long(left, right, side):
    left_top = left.astype(jnp.bfloat16)
    left_rest = left - left_top.astype(jnp.float32)
    right_top = right.astype(jnp.bfloat16)
    right_rest = right - right_top.astype(jnp.float32)
    small = short(left_top, right_rest, side) + short(left_rest, right_top, side)
    return small + short(left_top, right_top, side)


def halves(half):
    me_blk = lax.axis_index("blk")
    own = pl.ds(pl.multiple_of(me_blk * half, half), half)
    far = pl.ds(pl.multiple_of((1 - me_blk) * half, half), half)
    return me_blk, own, far


def own_kernel(mine_ref, matrix_ref, partial_ref, turned_ref=None):
    sub_dev, half, _ = mine_ref.shape
    _, own, _ = halves(half)
    for s in range(sub_dev):
        partial_ref[s] = jnp.dot(
            matrix_ref[s, :, own], mine_ref[s], preferred_element_type=jnp.float32
        )
        if turned_ref is not None:
            turned_ref[:, s * half : (s + 1) * half] = mine_ref[s].T


def far_kernel(
    counts_ref,
    stiff_own_ref,
    mass_own_ref,
    turned_ref,
    other_ref,
    stiff_ref,
    mass_ref,
    part_ref,
    keep_ref,
    send_ref,
    mass_part_ref,
):
    sub_dev, half, width = other_ref.shape
    me_blk, _, far = halves(half)
    first = me_blk == 0
    slot = me_blk * half + lax.broadcasted_iota(jnp.int32, (half, 1), 0)
    for s in range(sub_dev):
        part = mass_own_ref[s] + jnp.dot(
            mass_ref[s, :, far], other_ref[s], preferred_element_type=jnp.float32
        )
        mass_part_ref[s] = jnp.where(slot < counts_ref[s], part, 0.0).astype(jnp.bfloat16)
    for s in range(sub_dev):
        part = stiff_own_ref[s] + jnp.dot(
            stiff_ref[s, :, far], other_ref[s], preferred_element_type=jnp.float32
        )
        part_ref[s] = jnp.where(slot < counts_ref[s], part, 0.0).astype(jnp.bfloat16)
    for place, parts_ref in enumerate((mass_part_ref, part_ref)):
        parts = parts_ref[...].reshape(sub_dev * half, width)
        gram = jnp.dot(turned_ref[...], parts, preferred_element_type=jnp.float32)
        low, high = gram[: width // 2], gram[width // 2 :]
        keep_ref[place] = jnp.where(first, low, high)
        send_ref[place] = jnp.where(first, high, low)


def products(counts, mine, other, stiffness, mass):
    sub_dev, half, width = mine.shape
    vmem = pl.BlockSpec(memory_space=pltpu.VMEM)
    params = pltpu.CompilerParams(vmem_limit_bytes=20 << 20)
    partial = jax.ShapeDtypeStruct((sub_dev, half, width), jnp.float32)
    cost = pl.CostEstimate(flops=270000000, bytes_accessed=2 << 20, transcendentals=0)
    stiff_own, turned = pl.pallas_call(
        own_kernel,
        out_shape=(partial, jax.ShapeDtypeStruct((width, sub_dev * half), jnp.bfloat16)),
        in_specs=[vmem] * 2,
        out_specs=(vmem, vmem),
        compiler_params=params,
        cost_estimate=cost,
        name="own_stiff",
    )(mine, stiffness)
    mass_own = pl.pallas_call(
        own_kernel,
        out_shape=partial,
        in_specs=[vmem] * 2,
        out_specs=vmem,
        compiler_params=params,
        cost_estimate=cost,
        name="own_mass",
    )(mine, mass)
    gram = jax.ShapeDtypeStruct((2, width // 2, width), jnp.float32)
    return pl.pallas_call(
        far_kernel,
        out_shape=(jax.ShapeDtypeStruct(mine.shape, jnp.bfloat16), gram, gram),
        in_specs=[pl.BlockSpec(memory_space=pltpu.SMEM)] + [vmem] * 6,
        out_specs=(vmem, vmem, vmem),
        scratch_shapes=[pltpu.VMEM((sub_dev, half, width), jnp.bfloat16)],
        compiler_params=params,
        cost_estimate=pl.CostEstimate(flops=810000000, bytes_accessed=4 << 20, transcendentals=0),
        name="far_half",
    )(counts, stiff_own, mass_own, turned, other, stiffness, mass)


def eliminate(work_ref, inverse_ref):
    n = work_ref.shape[0]
    row = lax.broadcasted_iota(jnp.int32, (n, n), 0)
    col = lax.broadcasted_iota(jnp.int32, (n, n), 1)
    lane = lax.broadcasted_iota(jnp.int32, (1, n), 1)
    inverse_ref[...] = jnp.where(row == col, 1.0, 0.0)

    def column(k, _):
        pivot_row = work_ref[pl.ds(k, 1), :]
        pivot = jnp.sum(jnp.where(lane == k, pivot_row, 0.0), axis=1, keepdims=True)
        work = work_ref[...]
        inverse = inverse_ref[...]
        below = jnp.sum(jnp.where(col == k, work, 0.0), axis=1, keepdims=True) / pivot
        below = jnp.where(row[:, :1] > k, below, 0.0)
        inverse_row = inverse_ref[pl.ds(k, 1), :]
        work_ref[...] = work - below * pivot_row
        inverse = inverse - below * inverse_row
        inverse_ref[...] = jnp.where(row == k, inverse * lax.rsqrt(pivot), inverse)
        return 0

    lax.fori_loop(0, n, column, 0)


def join(target_ref, mine_ref, other_ref, plane):
    rows = mine_ref.shape[1]
    me_blk = lax.axis_index("blk")
    target_ref[pl.ds(pl.multiple_of(me_blk * rows, rows), rows), :] = mine_ref[plane]
    target_ref[pl.ds(pl.multiple_of((1 - me_blk) * rows, rows), rows), :] = other_ref[plane]


def inverse_kernel(mine_ref, other_ref, inverse_ref, gram_ref, rest_ref):
    n = mine_ref.shape[2]
    join(gram_ref, mine_ref, other_ref, 0)
    row = lax.broadcasted_iota(jnp.int32, (n, n), 0)
    col = lax.broadcasted_iota(jnp.int32, (n, n), 1)
    eye = jnp.where(row == col, 1.0, 0.0)
    weight = jnp.where(row > col, 1.0, 0.5 * eye)
    gram = gram_ref[...]
    gram = 0.5 * (gram + gram.T)
    gram_ref[...] = gram
    on_diag = jnp.where(row == col, gram, 0.0)
    down = lax.rsqrt(jnp.sum(on_diag, axis=1, keepdims=True))
    across = lax.rsqrt(jnp.sum(on_diag, axis=0, keepdims=True))
    rest = jnp.where(row == col, 0.0, gram * down * across)
    rest_ref[...] = rest
    lead = weight * rest
    off = weight * short(lead, lead, 1) + short(lead, lead, 0) - lead
    left = rest + off + short(off, rest, 0)
    step = weight * (left + off.T + short(left, off, 1))
    off = off - step - short(step, off, 0)
    inverse_ref[...] = off

    def going(state):
        step, size = state
        return jnp.logical_and(step < MAX_STEPS, jnp.logical_not(size < RESIDUAL))

    def correct(state):
        step, _ = state
        off = inverse_ref[...]
        rest = rest_ref[...]
        left = rest + off + long(off, rest, 0)
        error = left + off.T + long(left, off, 1)
        change = weight * error
        inverse_ref[...] = off - change - short(change, off, 0)
        return step + 1, jnp.sum(error * error)

    _, size = lax.while_loop(going, correct, (jnp.int32(0), jnp.float32(1.0)))
    inverse_ref[...] = (eye + inverse_ref[...]) * across

    @pl.when(jnp.logical_not(size < RESIDUAL))
    def _():
        eliminate(gram_ref, inverse_ref)


def rotate_kernel(
    scale,
    inverse_ref,
    mine_ref,
    other_ref,
    image_ref,
    extra_ref,
    rotated_hbm,
    projected_hbm,
    gram_ref,
    rotated_ref,
    projected_ref,
    sems,
):
    join(gram_ref, mine_ref, other_ref, 1)
    inverse = inverse_ref[...]
    rotated_ref[...] = scale * long(image_ref[...] + extra_ref[...], inverse, 1)
    first = pltpu.make_async_copy(rotated_ref, rotated_hbm, sems.at[0])
    first.start()
    projected_ref[...] = long(long(inverse, gram_ref[...], 0), inverse, 1)
    second = pltpu.make_async_copy(projected_ref, projected_hbm, sems.at[1])
    second.start()
    first.wait()
    second.wait()


def ritz(mine, other, image, extra, scale):
    n = mine.shape[2]
    vmem = pl.BlockSpec(memory_space=pltpu.VMEM)
    hbm = pl.BlockSpec(memory_space=pltpu.HBM)
    square = jax.ShapeDtypeStruct((n, n), jnp.float32)
    params = pltpu.CompilerParams(vmem_limit_bytes=16 << 20)
    spare = pltpu.VMEM((n, n), jnp.float32)
    inverse = pl.pallas_call(
        inverse_kernel,
        out_shape=square,
        in_specs=[vmem] * 2,
        out_specs=vmem,
        scratch_shapes=[spare, spare],
        compiler_params=params,
        cost_estimate=pl.CostEstimate(flops=3000000000, bytes_accessed=1 << 20, transcendentals=512),
        name="inverse",
    )(mine, other)
    return pl.pallas_call(
        functools.partial(rotate_kernel, scale),
        out_shape=(square, square),
        in_specs=[vmem] * 5,
        out_specs=(hbm, hbm),
        scratch_shapes=[spare, spare, spare, pltpu.SemaphoreType.DMA((2,))],
        compiler_params=params,
        name="rotate",
    )(inverse, mine, other, image, extra)


def to_pieces(planes):
    n, rows, wide = planes.shape
    pieces = planes.reshape(n, 2, rows // 2, 2, wide // 2).transpose(3, 2, 0, 1, 4)
    return pieces.reshape(rows, 2 * n, wide // 2)


def from_pieces(pieces):
    rows, double, lanes = pieces.shape
    planes = pieces.reshape(2, rows // 2, double // 2, 2, lanes).transpose(2, 3, 1, 0, 4)
    return planes.reshape(double // 2, rows, 2 * lanes)


def per_device(basis, stiffness, mass, owner_rows, counts):
    n_sub = lax.axis_size("sub")
    me_sub = lax.axis_index("sub")
    me_blk = lax.axis_index("blk")
    rows_dev, width = basis.shape
    sub_dev, half, order = stiffness.shape
    cap = owner_rows.shape[2]
    cap_half = cap // 2
    lanes = width // 2
    table = lax.dynamic_slice_in_dim(owner_rows[0], me_blk * cap_half, cap_half, 1)
    picks = select_rows(table.reshape(-1), rows_dev)

    sent = jnp.dot(picks, basis, preferred_element_type=jnp.float32).astype(jnp.bfloat16)
    sent, me_sub, me_blk = lax.optimization_barrier((sent, me_sub, me_blk))
    received = lax.all_to_all(
        sent.reshape(n_sub, cap_half, width), "sub", split_axis=0, concat_axis=0, tiled=True
    )
    received, counts, me_sub, me_blk = lax.optimization_barrier((received, counts, me_sub, me_blk))
    received = with_layout_constraint(received.transpose(1, 0, 2), Layout((0, 1, 2)))
    mine = jnp.roll(received, -me_sub, axis=1).reshape(sub_dev, half, width)
    slots = jnp.arange(half, dtype=jnp.int32)
    my_live = (slots[None, :] < (counts - me_blk * half)[:, None])[:, :, None]
    mine = jnp.where(my_live, mine, jnp.zeros((), jnp.bfloat16))
    other = lax.ppermute(mine, "blk", SWAP)
    stiff_part, keep, send = products(counts, mine, other, stiffness, mass)
    grams = keep + lax.ppermute(send, "blk", SWAP)
    terms = to_pieces(jnp.concatenate(two_terms(grams)))
    outgoing = stiff_part.reshape(cap_half, n_sub, width).transpose(1, 0, 2)
    outgoing = jnp.roll(outgoing, me_sub, axis=0)
    back = lax.all_to_all(
        jnp.concatenate([outgoing, terms], axis=2),
        "sub",
        split_axis=0,
        concat_axis=0,
        tiled=True,
    )
    total = jnp.sum(back[:, :, width:].astype(jnp.float32), axis=0)
    total = total[:4] + total[4:]
    spread = lax.all_to_all(
        jnp.broadcast_to(total[None], (n_sub, 4, lanes)),
        "sub",
        split_axis=0,
        concat_axis=0,
        tiled=True,
    )
    spread, back, me_blk = lax.optimization_barrier((spread, back, me_blk))
    mine_grams = from_pieces(spread)
    other_grams = lax.ppermute(mine_grams, "blk", SWAP)
    image = jnp.einsum(
        "tr,tc->rc",
        picks,
        back[:, :, :width].reshape(-1, width),
        preferred_element_type=jnp.float32,
    )
    rows_core = rows_dev // 2
    image_k = lax.dynamic_slice_in_dim(image, me_blk * rows_core, rows_core, 0)
    extra_k = lax.dynamic_slice_in_dim(image, (1 - me_blk) * rows_core, rows_core, 0)
    extra_k = lax.ppermute(extra_k, "blk", SWAP)
    return ritz(mine_grams, other_grams, image_k, extra_k, math.sqrt(rows_dev * n_sub))


def solution(mesh):
    return jax.shard_map(
        per_device,
        mesh=mesh,
        in_specs=(
            P("sub", None),
            P("sub", "blk", None),
            P("sub", "blk", None),
            P("sub", None, None),
            P("sub"),
        ),
        out_specs=(P(("sub", "blk"), None), P()),
        check_vma=False,
    )
```

```python
import functools
import math

import jax
import jax.numpy as jnp
from jax import lax
from jax.experimental.layout import Layout, with_layout_constraint
from jax.experimental import pallas as pl
from jax.experimental.pallas import tpu as pltpu
from jax.sharding import PartitionSpec as P

SWAP = ((0, 1), (1, 0))
MAX_STEPS = 7
RESIDUAL = 1e-6


def select_rows(index, count):
    places = lax.broadcasted_iota(jnp.int32, (index.shape[0], count), 1)
    return (index[:, None] == places).astype(jnp.bfloat16)


def two_terms(value):
    upper = lax.reduce_precision(value, exponent_bits=8, mantissa_bits=7)
    return upper.astype(jnp.bfloat16), (value - upper).astype(jnp.bfloat16)


def short(left, right, side):
    return lax.dot_general(
        left.astype(jnp.bfloat16),
        right.astype(jnp.bfloat16),
        (((1,), (side,)), ((), ())),
        preferred_element_type=jnp.float32,
    )


def long(left, right, side):
    left_top = left.astype(jnp.bfloat16)
    left_rest = left - left_top.astype(jnp.float32)
    right_top = right.astype(jnp.bfloat16)
    right_rest = right - right_top.astype(jnp.float32)
    small = short(left_top, right_rest, side) + short(left_rest, right_top, side)
    return small + short(left_top, right_top, side)


def halves(half):
    me_blk = lax.axis_index("blk")
    own = pl.ds(pl.multiple_of(me_blk * half, half), half)
    far = pl.ds(pl.multiple_of((1 - me_blk) * half, half), half)
    return me_blk, own, far


def own_kernel(mine_ref, matrix_ref, partial_ref, turned_ref=None):
    sub_dev, half, _ = mine_ref.shape
    _, own, _ = halves(half)
    for s in range(sub_dev):
        partial_ref[s] = jnp.dot(
            matrix_ref[s, :, own], mine_ref[s], preferred_element_type=jnp.float32
        )
        if turned_ref is not None:
            turned_ref[:, s * half : (s + 1) * half] = mine_ref[s].T


def far_kernel(
    counts_ref,
    stiff_own_ref,
    mass_own_ref,
    turned_ref,
    other_ref,
    stiff_ref,
    mass_ref,
    part_ref,
    keep_ref,
    send_ref,
    mass_part_ref,
):
    sub_dev, half, width = other_ref.shape
    me_blk, _, far = halves(half)
    first = me_blk == 0
    slot = me_blk * half + lax.broadcasted_iota(jnp.int32, (half, 1), 0)
    for s in range(sub_dev):
        part = mass_own_ref[s] + jnp.dot(
            mass_ref[s, :, far], other_ref[s], preferred_element_type=jnp.float32
        )
        mass_part_ref[s] = jnp.where(slot < counts_ref[s], part, 0.0).astype(jnp.bfloat16)
    for s in range(sub_dev):
        part = stiff_own_ref[s] + jnp.dot(
            stiff_ref[s, :, far], other_ref[s], preferred_element_type=jnp.float32
        )
        part_ref[s] = jnp.where(slot < counts_ref[s], part, 0.0).astype(jnp.bfloat16)
    for place, parts_ref in enumerate((mass_part_ref, part_ref)):
        parts = parts_ref[...].reshape(sub_dev * half, width)
        gram = jnp.dot(turned_ref[...], parts, preferred_element_type=jnp.float32)
        low, high = gram[: width // 2], gram[width // 2 :]
        keep_ref[place] = jnp.where(first, low, high)
        send_ref[place] = jnp.where(first, high, low)


def products(counts, mine, other, stiffness, mass):
    sub_dev, half, width = mine.shape
    vmem = pl.BlockSpec(memory_space=pltpu.VMEM)
    params = pltpu.CompilerParams(vmem_limit_bytes=20 << 20)
    partial = jax.ShapeDtypeStruct((sub_dev, half, width), jnp.float32)
    cost = pl.CostEstimate(flops=270000000, bytes_accessed=2 << 20, transcendentals=0)
    stiff_own, turned = pl.pallas_call(
        own_kernel,
        out_shape=(partial, jax.ShapeDtypeStruct((width, sub_dev * half), jnp.bfloat16)),
        in_specs=[vmem] * 2,
        out_specs=(vmem, vmem),
        compiler_params=params,
        cost_estimate=cost,
        name="own_stiff",
    )(mine, stiffness)
    mass_own = pl.pallas_call(
        own_kernel,
        out_shape=partial,
        in_specs=[vmem] * 2,
        out_specs=vmem,
        compiler_params=params,
        cost_estimate=cost,
        name="own_mass",
    )(mine, mass)
    gram = jax.ShapeDtypeStruct((2, width // 2, width), jnp.float32)
    return pl.pallas_call(
        far_kernel,
        out_shape=(jax.ShapeDtypeStruct(mine.shape, jnp.bfloat16), gram, gram),
        in_specs=[pl.BlockSpec(memory_space=pltpu.SMEM)] + [vmem] * 6,
        out_specs=(vmem, vmem, vmem),
        scratch_shapes=[pltpu.VMEM((sub_dev, half, width), jnp.bfloat16)],
        compiler_params=params,
        cost_estimate=pl.CostEstimate(flops=810000000, bytes_accessed=4 << 20, transcendentals=0),
        name="far_half",
    )(counts, stiff_own, mass_own, turned, other, stiffness, mass)


def eliminate(work_ref, inverse_ref):
    n = work_ref.shape[0]
    row = lax.broadcasted_iota(jnp.int32, (n, n), 0)
    col = lax.broadcasted_iota(jnp.int32, (n, n), 1)
    lane = lax.broadcasted_iota(jnp.int32, (1, n), 1)
    inverse_ref[...] = jnp.where(row == col, 1.0, 0.0)

    def column(k, _):
        pivot_row = work_ref[pl.ds(k, 1), :]
        pivot = jnp.sum(jnp.where(lane == k, pivot_row, 0.0), axis=1, keepdims=True)
        work = work_ref[...]
        inverse = inverse_ref[...]
        below = jnp.sum(jnp.where(col == k, work, 0.0), axis=1, keepdims=True) / pivot
        below = jnp.where(row[:, :1] > k, below, 0.0)
        inverse_row = inverse_ref[pl.ds(k, 1), :]
        work_ref[...] = work - below * pivot_row
        inverse = inverse - below * inverse_row
        inverse_ref[...] = jnp.where(row == k, inverse * lax.rsqrt(pivot), inverse)
        return 0

    lax.fori_loop(0, n, column, 0)


def join(target_ref, mine_ref, other_ref, plane):
    pieces, _, lanes = mine_ref.shape
    rows = pieces // 2
    me_blk = lax.axis_index("blk")
    for side, ref in ((me_blk, mine_ref), (1 - me_blk, other_ref)):
        for r in range(2):
            start = pl.multiple_of(side * pieces + r * rows, rows)
            for part in range(2):
                target_ref[pl.ds(start, rows), part * lanes : (part + 1) * lanes] = ref[
                    part * rows : (part + 1) * rows, 2 * plane + r, :
                ]


def inverse_kernel(mine_ref, other_ref, inverse_ref, gram_ref, rest_ref):
    n = gram_ref.shape[0]
    join(gram_ref, mine_ref, other_ref, 0)
    row = lax.broadcasted_iota(jnp.int32, (n, n), 0)
    col = lax.broadcasted_iota(jnp.int32, (n, n), 1)
    eye = jnp.where(row == col, 1.0, 0.0)
    weight = jnp.where(row > col, 1.0, 0.5 * eye)
    gram = gram_ref[...]
    gram = 0.5 * (gram + gram.T)
    gram_ref[...] = gram
    on_diag = jnp.where(row == col, gram, 0.0)
    down = lax.rsqrt(jnp.sum(on_diag, axis=1, keepdims=True))
    across = lax.rsqrt(jnp.sum(on_diag, axis=0, keepdims=True))
    rest = jnp.where(row == col, 0.0, gram * down * across)
    rest_ref[...] = rest
    lead = weight * rest
    off = weight * short(lead, lead, 1) + short(lead, lead, 0) - lead
    left = rest + off + short(off, rest, 0)
    step = weight * (left + off.T + short(left, off, 1))
    off = off - step - short(step, off, 0)
    inverse_ref[...] = off

    def going(state):
        step, size = state
        return jnp.logical_and(step < MAX_STEPS, jnp.logical_not(size < RESIDUAL))

    def correct(state):
        step, _ = state
        off = inverse_ref[...]
        rest = rest_ref[...]
        left = rest + off + long(off, rest, 0)
        error = left + off.T + long(left, off, 1)
        change = weight * error
        inverse_ref[...] = off - change - short(change, off, 0)
        return step + 1, jnp.sum(error * error)

    _, size = lax.while_loop(going, correct, (jnp.int32(0), jnp.float32(1.0)))
    inverse_ref[...] = (eye + inverse_ref[...]) * across

    @pl.when(jnp.logical_not(size < RESIDUAL))
    def _():
        eliminate(gram_ref, inverse_ref)


def rotate_kernel(
    scale,
    inverse_ref,
    mine_ref,
    other_ref,
    image_ref,
    extra_ref,
    rotated_hbm,
    projected_hbm,
    gram_ref,
    rotated_ref,
    projected_ref,
    sems,
):
    join(gram_ref, mine_ref, other_ref, 1)
    inverse = inverse_ref[...]
    rotated_ref[...] = scale * long(image_ref[...] + extra_ref[...], inverse, 1)
    first = pltpu.make_async_copy(rotated_ref, rotated_hbm, sems.at[0])
    first.start()
    projected_ref[...] = long(long(inverse, gram_ref[...], 0), inverse, 1)
    second = pltpu.make_async_copy(projected_ref, projected_hbm, sems.at[1])
    second.start()
    first.wait()
    second.wait()


def ritz(mine, other, image, extra, scale):
    n = image.shape[1]
    vmem = pl.BlockSpec(memory_space=pltpu.VMEM)
    hbm = pl.BlockSpec(memory_space=pltpu.HBM)
    square = jax.ShapeDtypeStruct((n, n), jnp.float32)
    params = pltpu.CompilerParams(vmem_limit_bytes=16 << 20)
    spare = pltpu.VMEM((n, n), jnp.float32)
    inverse = pl.pallas_call(
        inverse_kernel,
        out_shape=square,
        in_specs=[vmem] * 2,
        out_specs=vmem,
        scratch_shapes=[spare, spare],
        compiler_params=params,
        cost_estimate=pl.CostEstimate(flops=3000000000, bytes_accessed=1 << 20, transcendentals=512),
        name="inverse",
    )(mine, other)
    return pl.pallas_call(
        functools.partial(rotate_kernel, scale),
        out_shape=(square, square),
        in_specs=[vmem] * 5,
        out_specs=(hbm, hbm),
        scratch_shapes=[spare, spare, spare, pltpu.SemaphoreType.DMA((2,))],
        compiler_params=params,
        name="rotate",
    )(inverse, mine, other, image, extra)


def to_pieces(planes):
    n, rows, wide = planes.shape
    pieces = planes.reshape(n, 2, rows // 2, 2, wide // 2).transpose(3, 2, 0, 1, 4)
    return pieces.reshape(rows, 2 * n, wide // 2)


def per_device(basis, stiffness, mass, owner_rows, counts):
    n_sub = lax.axis_size("sub")
    me_sub = lax.axis_index("sub")
    me_blk = lax.axis_index("blk")
    rows_dev, width = basis.shape
    sub_dev, half, order = stiffness.shape
    cap = owner_rows.shape[2]
    cap_half = cap // 2
    lanes = width // 2
    table = lax.dynamic_slice_in_dim(owner_rows[0], me_blk * cap_half, cap_half, 1)
    picks = select_rows(table.reshape(-1), rows_dev)

    sent = jnp.dot(picks, basis, preferred_element_type=jnp.float32).astype(jnp.bfloat16)
    sent, me_sub, me_blk = lax.optimization_barrier((sent, me_sub, me_blk))
    received = lax.all_to_all(
        sent.reshape(n_sub, cap_half, width), "sub", split_axis=0, concat_axis=0, tiled=True
    )
    received, counts, me_sub, me_blk = lax.optimization_barrier((received, counts, me_sub, me_blk))
    received = with_layout_constraint(received.transpose(1, 0, 2), Layout((0, 1, 2)))
    mine = jnp.roll(received, -me_sub, axis=1).reshape(sub_dev, half, width)
    slots = jnp.arange(half, dtype=jnp.int32)
    my_live = (slots[None, :] < (counts - me_blk * half)[:, None])[:, :, None]
    mine = jnp.where(my_live, mine, jnp.zeros((), jnp.bfloat16))
    other = lax.ppermute(mine, "blk", SWAP)
    stiff_part, keep, send = products(counts, mine, other, stiffness, mass)
    grams = keep + lax.ppermute(send, "blk", SWAP)
    terms = to_pieces(jnp.concatenate(two_terms(grams)))
    outgoing = stiff_part.reshape(cap_half, n_sub, width).transpose(1, 0, 2)
    outgoing = jnp.roll(outgoing, me_sub, axis=0)
    back = lax.all_to_all(
        jnp.concatenate([outgoing, terms], axis=2),
        "sub",
        split_axis=0,
        concat_axis=0,
        tiled=True,
    )
    total = jnp.sum(back[:, :, width:].astype(jnp.float32), axis=0)
    total = total[:4] + total[4:]
    spread = lax.all_to_all(
        jnp.broadcast_to(total[None], (n_sub, 4, lanes)),
        "sub",
        split_axis=0,
        concat_axis=0,
        tiled=True,
    )
    spread, back, me_blk = lax.optimization_barrier((spread, back, me_blk))
    other_grams = lax.ppermute(spread, "blk", SWAP)

    image = jnp.einsum(
        "tr,tc->rc",
        picks,
        back[:, :, :width].reshape(-1, width),
        preferred_element_type=jnp.float32,
    )
    rows_core = rows_dev // 2
    image_k = lax.dynamic_slice_in_dim(image, me_blk * rows_core, rows_core, 0)
    extra_k = lax.dynamic_slice_in_dim(image, (1 - me_blk) * rows_core, rows_core, 0)
    extra_k = lax.ppermute(extra_k, "blk", SWAP)
    return ritz(spread, other_grams, image_k, extra_k, math.sqrt(rows_dev * n_sub))


def solution(mesh):
    return jax.shard_map(
        per_device,
        mesh=mesh,
        in_specs=(
            P("sub", None),
            P("sub", "blk", None),
            P("sub", "blk", None),
            P("sub", None, None),
            P("sub"),
        ),
        out_specs=(P(("sub", "blk"), None), P()),
        check_vma=False,
    )
```

```python
import functools
import math

import jax
import jax.numpy as jnp
from jax import lax
from jax.experimental.layout import Layout, with_layout_constraint
from jax.experimental import pallas as pl
from jax.experimental.pallas import tpu as pltpu
from jax.sharding import PartitionSpec as P

SWAP = ((0, 1), (1, 0))
MAX_STEPS = 7
RESIDUAL = 1e-6


def select_rows(index, count):
    places = lax.broadcasted_iota(jnp.int32, (index.shape[0], count), 1)
    return (index[:, None] == places).astype(jnp.bfloat16)


def two_terms(value):
    upper = lax.reduce_precision(value, exponent_bits=8, mantissa_bits=7)
    return upper.astype(jnp.bfloat16), (value - upper).astype(jnp.bfloat16)


def short(left, right, side):
    return lax.dot_general(
        left.astype(jnp.bfloat16),
        right.astype(jnp.bfloat16),
        (((1,), (side,)), ((), ())),
        preferred_element_type=jnp.float32,
    )


def long(left, right, side):
    left_top = left.astype(jnp.bfloat16)
    left_rest = left - left_top.astype(jnp.float32)
    right_top = right.astype(jnp.bfloat16)
    right_rest = right - right_top.astype(jnp.float32)
    small = short(left_top, right_rest, side) + short(left_rest, right_top, side)
    return small + short(left_top, right_top, side)


def halves(half):
    me_blk = lax.axis_index("blk")
    own = pl.ds(pl.multiple_of(me_blk * half, half), half)
    far = pl.ds(pl.multiple_of((1 - me_blk) * half, half), half)
    return me_blk, own, far


def own_kernel(mine_ref, matrix_ref, partial_ref, turned_ref=None):
    sub_dev, half, _ = mine_ref.shape
    _, own, _ = halves(half)
    for s in range(sub_dev):
        partial_ref[s] = jnp.dot(
            matrix_ref[s, :, own], mine_ref[s], preferred_element_type=jnp.float32
        )
        if turned_ref is not None:
            turned_ref[:, s * half : (s + 1) * half] = mine_ref[s].T


def scatter_pieces(target_ref, plane_rows, place):
    pieces, _, lanes = target_ref.shape
    rows = pieces // 2
    for r in range(2):
        for part in range(2):
            target_ref[part * rows : (part + 1) * rows, 2 * place + r, :] = plane_rows[
                r * rows : (r + 1) * rows, part * lanes : (part + 1) * lanes
            ]


def far_kernel(
    counts_ref,
    stiff_own_ref,
    mass_own_ref,
    turned_ref,
    other_ref,
    stiff_ref,
    mass_ref,
    part_ref,
    keep_ref,
    send_ref,
    mass_part_ref,
):
    sub_dev, half, width = other_ref.shape
    me_blk, _, far = halves(half)
    first = me_blk == 0
    slot = me_blk * half + lax.broadcasted_iota(jnp.int32, (half, 1), 0)
    for s in range(sub_dev):
        part = mass_own_ref[s] + jnp.dot(
            mass_ref[s, :, far], other_ref[s], preferred_element_type=jnp.float32
        )
        mass_part_ref[s] = jnp.where(slot < counts_ref[s], part, 0.0).astype(jnp.bfloat16)
    for s in range(sub_dev):
        part = stiff_own_ref[s] + jnp.dot(
            stiff_ref[s, :, far], other_ref[s], preferred_element_type=jnp.float32
        )
        part_ref[s] = jnp.where(slot < counts_ref[s], part, 0.0).astype(jnp.bfloat16)
    for place, parts_ref in enumerate((mass_part_ref, part_ref)):
        parts = parts_ref[...].reshape(sub_dev * half, width)
        gram = jnp.dot(turned_ref[...], parts, preferred_element_type=jnp.float32)
        low, high = gram[: width // 2], gram[width // 2 :]
        scatter_pieces(keep_ref, jnp.where(first, low, high), place)
        scatter_pieces(send_ref, jnp.where(first, high, low), place)


def products(counts, mine, other, stiffness, mass):
    sub_dev, half, width = mine.shape
    vmem = pl.BlockSpec(memory_space=pltpu.VMEM)
    params = pltpu.CompilerParams(vmem_limit_bytes=20 << 20)
    partial = jax.ShapeDtypeStruct((sub_dev, half, width), jnp.float32)
    cost = pl.CostEstimate(flops=270000000, bytes_accessed=2 << 20, transcendentals=0)
    stiff_own, turned = pl.pallas_call(
        own_kernel,
        out_shape=(partial, jax.ShapeDtypeStruct((width, sub_dev * half), jnp.bfloat16)),
        in_specs=[vmem] * 2,
        out_specs=(vmem, vmem),
        compiler_params=params,
        cost_estimate=cost,
        name="own_stiff",
    )(mine, stiffness)
    mass_own = pl.pallas_call(
        own_kernel,
        out_shape=partial,
        in_specs=[vmem] * 2,
        out_specs=vmem,
        compiler_params=params,
        cost_estimate=cost,
        name="own_mass",
    )(mine, mass)
    gram = jax.ShapeDtypeStruct((width // 2, 4, width // 2), jnp.float32)
    return pl.pallas_call(
        far_kernel,
        out_shape=(jax.ShapeDtypeStruct(mine.shape, jnp.bfloat16), gram, gram),
        in_specs=[pl.BlockSpec(memory_space=pltpu.SMEM)] + [vmem] * 6,
        out_specs=(vmem, vmem, vmem),
        scratch_shapes=[pltpu.VMEM((sub_dev, half, width), jnp.bfloat16)],
        compiler_params=params,
        cost_estimate=pl.CostEstimate(flops=810000000, bytes_accessed=4 << 20, transcendentals=0),
        name="far_half",
    )(counts, stiff_own, mass_own, turned, other, stiffness, mass)


def eliminate(work_ref, inverse_ref):
    n = work_ref.shape[0]
    row = lax.broadcasted_iota(jnp.int32, (n, n), 0)
    col = lax.broadcasted_iota(jnp.int32, (n, n), 1)
    lane = lax.broadcasted_iota(jnp.int32, (1, n), 1)
    inverse_ref[...] = jnp.where(row == col, 1.0, 0.0)

    def column(k, _):
        pivot_row = work_ref[pl.ds(k, 1), :]
        pivot = jnp.sum(jnp.where(lane == k, pivot_row, 0.0), axis=1, keepdims=True)
        work = work_ref[...]
        inverse = inverse_ref[...]
        below = jnp.sum(jnp.where(col == k, work, 0.0), axis=1, keepdims=True) / pivot
        below = jnp.where(row[:, :1] > k, below, 0.0)
        inverse_row = inverse_ref[pl.ds(k, 1), :]
        work_ref[...] = work - below * pivot_row
        inverse = inverse - below * inverse_row
        inverse_ref[...] = jnp.where(row == k, inverse * lax.rsqrt(pivot), inverse)
        return 0

    lax.fori_loop(0, n, column, 0)


def join(target_ref, mine_ref, other_ref, plane):
    pieces, _, lanes = mine_ref.shape
    rows = pieces // 2
    me_blk = lax.axis_index("blk")
    for side, ref in ((me_blk, mine_ref), (1 - me_blk, other_ref)):
        for r in range(2):
            start = pl.multiple_of(side * pieces + r * rows, rows)
            for part in range(2):
                target_ref[pl.ds(start, rows), part * lanes : (part + 1) * lanes] = ref[
                    part * rows : (part + 1) * rows, 2 * plane + r, :
                ]


def inverse_kernel(mine_ref, other_ref, inverse_ref, gram_ref, rest_ref):
    n = gram_ref.shape[0]
    join(gram_ref, mine_ref, other_ref, 0)
    row = lax.broadcasted_iota(jnp.int32, (n, n), 0)
    col = lax.broadcasted_iota(jnp.int32, (n, n), 1)
    eye = jnp.where(row == col, 1.0, 0.0)
    weight = jnp.where(row > col, 1.0, 0.5 * eye)
    gram = gram_ref[...]
    gram = 0.5 * (gram + gram.T)
    gram_ref[...] = gram
    on_diag = jnp.where(row == col, gram, 0.0)
    down = lax.rsqrt(jnp.sum(on_diag, axis=1, keepdims=True))
    across = lax.rsqrt(jnp.sum(on_diag, axis=0, keepdims=True))
    rest = jnp.where(row == col, 0.0, gram * down * across)
    rest_ref[...] = rest
    lead = weight * rest
    off = weight * short(lead, lead, 1) + short(lead, lead, 0) - lead
    left = rest + off + short(off, rest, 0)
    step = weight * (left + off.T + short(left, off, 1))
    off = off - step - short(step, off, 0)
    inverse_ref[...] = off

    def going(state):
        step, size = state
        return jnp.logical_and(step < MAX_STEPS, jnp.logical_not(size < RESIDUAL))

    def correct(state):
        step, _ = state
        off = inverse_ref[...]
        rest = rest_ref[...]
        left = rest + off + long(off, rest, 0)
        error = left + off.T + long(left, off, 1)
        change = weight * error
        inverse_ref[...] = off - change - short(change, off, 0)
        return step + 1, jnp.sum(error * error)

    _, size = lax.while_loop(going, correct, (jnp.int32(0), jnp.float32(1.0)))
    inverse_ref[...] = (eye + inverse_ref[...]) * across

    @pl.when(jnp.logical_not(size < RESIDUAL))
    def _():
        eliminate(gram_ref, inverse_ref)


def rotate_kernel(
    scale,
    inverse_ref,
    mine_ref,
    other_ref,
    image_ref,
    extra_ref,
    rotated_hbm,
    projected_hbm,
    gram_ref,
    rotated_ref,
    projected_ref,
    sems,
):
    join(gram_ref, mine_ref, other_ref, 1)
    inverse = inverse_ref[...]
    rotated_ref[...] = scale * long(image_ref[...] + extra_ref[...], inverse, 1)
    first = pltpu.make_async_copy(rotated_ref, rotated_hbm, sems.at[0])
    first.start()
    projected_ref[...] = long(long(inverse, gram_ref[...], 0), inverse, 1)
    second = pltpu.make_async_copy(projected_ref, projected_hbm, sems.at[1])
    second.start()
    first.wait()
    second.wait()


def ritz(mine, other, image, extra, scale):
    n = image.shape[1]
    vmem = pl.BlockSpec(memory_space=pltpu.VMEM)
    hbm = pl.BlockSpec(memory_space=pltpu.HBM)
    square = jax.ShapeDtypeStruct((n, n), jnp.float32)
    params = pltpu.CompilerParams(vmem_limit_bytes=16 << 20)
    spare = pltpu.VMEM((n, n), jnp.float32)
    inverse = pl.pallas_call(
        inverse_kernel,
        out_shape=square,
        in_specs=[vmem] * 2,
        out_specs=vmem,
        scratch_shapes=[spare, spare],
        compiler_params=params,
        cost_estimate=pl.CostEstimate(flops=3000000000, bytes_accessed=1 << 20, transcendentals=512),
        name="inverse",
    )(mine, other)
    return pl.pallas_call(
        functools.partial(rotate_kernel, scale),
        out_shape=(square, square),
        in_specs=[vmem] * 5,
        out_specs=(hbm, hbm),
        scratch_shapes=[spare, spare, spare, pltpu.SemaphoreType.DMA((2,))],
        compiler_params=params,
        name="rotate",
    )(inverse, mine, other, image, extra)


def per_device(basis, stiffness, mass, owner_rows, counts):
    n_sub = lax.axis_size("sub")
    me_sub = lax.axis_index("sub")
    me_blk = lax.axis_index("blk")
    rows_dev, width = basis.shape
    sub_dev, half, order = stiffness.shape
    cap = owner_rows.shape[2]
    cap_half = cap // 2
    lanes = width // 2
    table = lax.dynamic_slice_in_dim(owner_rows[0], me_blk * cap_half, cap_half, 1)
    picks = select_rows(table.reshape(-1), rows_dev)

    sent = jnp.dot(picks, basis, preferred_element_type=jnp.float32).astype(jnp.bfloat16)
    sent, me_sub, me_blk = lax.optimization_barrier((sent, me_sub, me_blk))
    received = lax.all_to_all(
        sent.reshape(n_sub, cap_half, width), "sub", split_axis=0, concat_axis=0, tiled=True
    )
    received, counts, me_sub, me_blk = lax.optimization_barrier((received, counts, me_sub, me_blk))
    received = with_layout_constraint(received.transpose(1, 0, 2), Layout((0, 1, 2)))
    mine = jnp.roll(received, -me_sub, axis=1).reshape(sub_dev, half, width)
    slots = jnp.arange(half, dtype=jnp.int32)
    my_live = (slots[None, :] < (counts - me_blk * half)[:, None])[:, :, None]
    mine = jnp.where(my_live, mine, jnp.zeros((), jnp.bfloat16))
    other = lax.ppermute(mine, "blk", SWAP)
    stiff_part, keep, send = products(counts, mine, other, stiffness, mass)
    grams = keep + lax.ppermute(send, "blk", SWAP)
    terms = jnp.concatenate(two_terms(grams), axis=1)
    outgoing = stiff_part.reshape(cap_half, n_sub, width).transpose(1, 0, 2)
    outgoing = jnp.roll(outgoing, me_sub, axis=0)
    back = lax.all_to_all(
        jnp.concatenate([outgoing, terms], axis=2),
        "sub",
        split_axis=0,
        concat_axis=0,
        tiled=True,
    )
    total = jnp.sum(back[:, :, width:].astype(jnp.float32), axis=0)
    total = total[:4] + total[4:]
    spread = lax.all_to_all(
        jnp.broadcast_to(total[None], (n_sub, 4, lanes)),
        "sub",
        split_axis=0,
        concat_axis=0,
        tiled=True,
    )
    spread, back, me_blk = lax.optimization_barrier((spread, back, me_blk))
    other_grams = lax.ppermute(spread, "blk", SWAP)

    image = jnp.einsum(
        "tr,tc->rc",
        picks,
        back[:, :, :width].reshape(-1, width),
        preferred_element_type=jnp.float32,
    )
    rows_core = rows_dev // 2
    image_k = lax.dynamic_slice_in_dim(image, me_blk * rows_core, rows_core, 0)
    extra_k = lax.dynamic_slice_in_dim(image, (1 - me_blk) * rows_core, rows_core, 0)
    extra_k = lax.ppermute(extra_k, "blk", SWAP)
    return ritz(spread, other_grams, image_k, extra_k, math.sqrt(rows_dev * n_sub))


def solution(mesh):
    return jax.shard_map(
        per_device,
        mesh=mesh,
        in_specs=(
            P("sub", None),
            P("sub", "blk", None),
            P("sub", "blk", None),
            P("sub", None, None),
            P("sub"),
        ),
        out_specs=(P(("sub", "blk"), None), P()),
        check_vma=False,
    )
```
